32 devices in a mesh: blk: 8 (over z, y), lblk: 4 (over x, core).
Axes of the slice: x: 2, y: 2, z: 4, core: 2. Of those that a mesh axis runs over, the one named last changes fastest.
Arguments:
- sky: bfloat16 [8, 2, 32, 16384], P(None, None, 'blk', 'lblk'), may hold values from -6 to 6
- arc_start: int32 [2, 32], P(None, 'blk'), may hold values from 0 to 16383
- arc_count: int32 [2, 32], P(None, 'blk'), may hold values from 4096 to 16384
- owner_modes: int32 [32], replicated, may hold values from 0 to 31, each once
- legendre: bfloat16 [32, 8, 4, 4096], P('blk', None, None, 'lblk'), may hold values from -1 to 1
Outputs:
- alm: float32 [8, 2, 32, 4096], P(None, None, 'blk', 'lblk')
The draws below stay inside these ranges and needn't reach their ends.
Inputs may be any that keep to these rules, and one draw needn't show every extreme that they name: `owner_modes`: each m-mode 0 to 31 appears exactly once.
All inputs are finite; a program needn't handle non-finite values.
Results may differ from the reference program's by a relative error of at most 0.0049.
Values may be sent and summed in bfloat16 or wider, within the bound.
No kernel may reach another device: no remote copies, remote signals or barrier semaphores. Data moves between devices by JAX's collectives and lax.ppermute only.
A program may use at most 64 MiB of HBM per device.

```python
import math
import jax
import jax.numpy as jnp
from jax import lax

RLEN = 16384
L = 4096
CYCLE_DEV = 4
MAPS = 8
M_SLAB = 32
CYCLES_HALF = 32


def plant(result, stream_key, smallest, largest):
    extent = result.shape
    place = [jax.random.randint(jax.random.fold_in(stream_key, axis), (), 0, extent[axis]) for axis in range(len(extent))]
    result = result.at[tuple(place)].set(smallest)
    longest = extent.index(max(extent))
    place[longest] = (place[longest] + 1) % extent[longest]
    return result.at[tuple(place)].set(largest)


def steps_of(stream_key, dims, cuts, smallest, high):
    factor_of = 1.0
    for dim, blocks in cuts:
        heights = jax.random.uniform(jax.random.fold_in(jax.random.fold_in(stream_key, 6), dim), (blocks,), jnp.float32, smallest / len(cuts), high / len(cuts))
        factor_of = factor_of * jnp.repeat(jnp.exp(heights), dims[dim] // blocks).reshape((-1,) + (1,) * (len(dims) - 1 - dim))
    return factor_of


def normal_values(stream_key, extent, spread, bound, shards=(), kind=jnp.bfloat16):
    result = spread * jax.random.normal(stream_key, extent, jnp.float32)
    if shards:
        result = result * steps_of(stream_key, extent, shards, -0.22, 0.18)
    return jnp.clip(result, -bound, bound).astype(kind)


def setup_inputs(seed: int = 0) -> dict:
    key_list = jax.random.split(jax.random.key(seed), 6)
    return {
        "sky": normal_values(key_list[0], (MAPS, 2, CYCLES_HALF, RLEN), 1.0, 6.0, ((2, 8), (3, 4))),
        "arc_start": plant(jax.random.randint(key_list[1], (2, CYCLES_HALF), 0, RLEN), jax.random.fold_in(key_list[1], 1), 0, RLEN - 1).astype(jnp.int32),
        "arc_count": plant(jax.random.randint(key_list[2], (2, CYCLES_HALF), RLEN // 4, RLEN + 1), jax.random.fold_in(key_list[2], 1), RLEN // 4, RLEN).astype(jnp.int32),
        "owner_modes": jax.random.permutation(key_list[3], M_SLAB).astype(jnp.int32),
        "legendre": normal_values(key_list[4], (M_SLAB, CYCLES_HALF // CYCLE_DEV, CYCLE_DEV, L), CYCLES_HALF ** -0.5, 1.0, ((0, 8), (3, 4))),
    }


DIFFUSION = 0.2

def mode_basis(positions, mode_list):
    product_index = jnp.mod(positions[:, None] * mode_list[None, :], RLEN)
    angles = 2.0 * math.pi / RLEN * product_index.astype(jnp.float32)
    return (jnp.cos(angles).astype(jnp.bfloat16), (-jnp.sin(angles)).astype(jnp.bfloat16))

def smooth_map(one_map, arc_start, arc_count):
    pixels = jnp.arange(RLEN, dtype=jnp.int32)
    offset = jnp.mod(pixels[None, None, :] - arc_start[:, :, None], RLEN)
    kept_mask = offset < arc_count[:, :, None]
    centre = jnp.where(kept_mask, one_map, jnp.zeros((), one_map.dtype)).astype(jnp.float32)
    zero_row = jnp.zeros_like(centre[:, :1])
    layer_above = jnp.concatenate([zero_row, centre[:, :-1]], axis=1)
    layer_below = jnp.concatenate([centre[:, 1:], centre[::-1, -1:]], axis=1)
    pixel_before = jnp.roll(centre, 1, axis=2)
    pixel_after = jnp.roll(centre, -1, axis=2)
    total = layer_above + layer_below + pixel_before + pixel_after - 4.0 * centre
    return (centre + DIFFUSION * total).astype(jnp.bfloat16)

def reference(sky, arc_start, arc_count, owner_modes, legendre):
    pixels = jnp.arange(RLEN, dtype=jnp.int32)
    cos_table, sin_table = mode_basis(pixels, owner_modes)
    parity = jnp.arange(CYCLES_HALF, dtype=jnp.int32) % 2
    phase_turn = math.pi / RLEN * (parity[:, None] * owner_modes[None, :]).astype(jnp.float32)
    turn_cos = jnp.cos(phase_turn)
    turn_sin = jnp.sin(phase_turn)
    norm_scale = 1.0 / math.sqrt(RLEN)

    def fourier_map(one_map):
        smooth = smooth_map(one_map, arc_start, arc_count)
        flat_rows = smooth.reshape(-1, RLEN)
        real_part = jnp.dot(flat_rows, cos_table, preferred_element_type=jnp.float32).reshape(2, CYCLES_HALF, -1)
        imag_part = jnp.dot(flat_rows, sin_table, preferred_element_type=jnp.float32).reshape(2, CYCLES_HALF, -1)
        rotated_real = (real_part * turn_cos + imag_part * turn_sin) * norm_scale
        rotated_imag = (imag_part * turn_cos - real_part * turn_sin) * norm_scale
        return jnp.stack([rotated_real, rotated_imag], axis=2).astype(jnp.bfloat16)
    fourier = lax.map(fourier_map, sky)
    north_part = fourier[:, 0].astype(jnp.float32)
    south_part = fourier[:, 1].astype(jnp.float32)
    folded = jnp.concatenate([north_part + south_part, north_part - south_part], axis=2).astype(jnp.bfloat16)
    degrees = jnp.arange(L, dtype=jnp.int32)

    def mode_section(inputs):
        block, folded_mode, mode = inputs
        legendre_rows = block.reshape(-1, L).astype(jnp.float32)
        latitude_sums = jnp.einsum('xry,rl->xyl', folded_mode.astype(jnp.float32), legendre_rows, precision=lax.Precision.HIGHEST)
        even_parity = jnp.mod(degrees + mode, 2) == 0
        chosen = jnp.where(even_parity[None, None, :], latitude_sums[:, :2], latitude_sums[:, 2:])
        return jnp.where((degrees >= mode)[None, None, :], chosen, jnp.zeros((), jnp.float32))
    stacked = lax.map(mode_section, (legendre, jnp.moveaxis(folded, 3, 0), owner_modes))
    return jnp.transpose(stacked, (1, 2, 0, 3))
```

```python
import math

import jax
import jax.numpy as jnp
from jax import lax
from jax.experimental import pallas as pl
from jax.experimental.pallas import tpu as pltpu
from jax.sharding import PartitionSpec as P

DIFFUSION = 0.2
LANES = 128

COS_TERMS = (1.0, -1.0 / 2, 1.0 / 24, -1.0 / 720, 1.0 / 40320, -1.0 / 3628800)
SIN_TERMS = (1.0, -1.0 / 6, 1.0 / 120, -1.0 / 5040, 1.0 / 362880)


def horner(terms, square):
    total = jnp.full_like(square, terms[-1])
    for term in terms[-2::-1]:
        total = total * square + term
    return total


def circle(index, turn):
    index = index & (turn - 1)
    quadrant = (index * 4 + turn // 2) >> (turn.bit_length() - 1)
    rest = (index - quadrant * (turn // 4)).astype(jnp.float32) * (2.0 * math.pi / turn)
    square = rest * rest
    cosine = horner(COS_TERMS, square)
    sine = rest * horner(SIN_TERMS, square)
    odd = (quadrant & 1) == 1
    swapped_cos = jnp.where(odd, sine, cosine)
    swapped_sin = jnp.where(odd, cosine, sine)
    cos_sign = ((quadrant + 1) & 2) == 2
    sin_sign = (quadrant & 2) == 2
    return (
        jnp.where(cos_sign, -swapped_cos, swapped_cos),
        jnp.where(sin_sign, -swapped_sin, swapped_sin),
    )


def iota(shape, axis):
    return lax.broadcasted_iota(jnp.int32, shape, axis)


def fourier_kernel(maps, band, quarter, ring, owned, copies, chunk, chunks):
    pieces = quarter // LANES
    rows = 2 * pieces * band

    def body(sky_hbm, start_hbm, count_hbm, modes_hbm, flat_hbm, out_ref, aux_ref, sky_ref, start_ref, count_ref, modes_ref, flat_ref, sems, sky_sems):
        small = [
            pltpu.make_async_copy(modes_hbm, modes_ref, sems.at[0]),
            pltpu.make_async_copy(flat_hbm, flat_ref, sems.at[1]),
            pltpu.make_async_copy(start_hbm, start_ref, sems.at[2]),
            pltpu.make_async_copy(count_hbm, count_ref, sems.at[3]),
        ]
        for copy in small:
            copy.start()
        sky_copies = [
            pltpu.make_async_copy(
                sky_hbm.at[pl.ds(x * rows, rows)], sky_ref.at[pl.ds(x * rows, rows)], sky_sems.at[x]
            )
            for x in range(maps)
        ]
        for copy in sky_copies:
            copy.start()
        first_pixel = lax.axis_index("lblk") * quarter
        block = lax.axis_index("blk")
        for copy in small:
            copy.wait()

        row = iota((8, LANES), 0) % owned
        lane = iota((8, LANES), 1)
        mine = jnp.zeros((8, LANES), jnp.int32)
        for s in range(owned):
            mine = jnp.where(row == s, flat_ref[block * owned + s], mine)
        scale = DIFFUSION / math.sqrt(ring)
        step_cos, _ = circle(mine, ring)
        turn_cos, turn_sin = circle(mine * (lane % band % 2), 2 * ring)
        aux_ref[0] = scale * (1.0 + 2.0 * step_cos)
        aux_ref[1] = turn_cos
        aux_ref[2] = jnp.where(lane < LANES // 2, turn_sin, -turn_sin)
        aux_ref[3] = mine.astype(jnp.float32)

        masks = []
        row8 = iota((8, LANES), 0)
        lane8 = iota((8, LANES), 1)
        for h in range(2):
            start = jnp.zeros((8, LANES), jnp.int32)
            count = jnp.zeros((8, LANES), jnp.int32)
            for k in range(band):
                start = jnp.where(row8 % band == k, start_ref[h, k], start)
                count = jnp.where(row8 % band == k, count_ref[h, k], count)
            shifted = first_pixel + (row8 // band) * LANES + lane8 - start
            for t in range(pieces * band // 8):
                offset = (shifted + t * (8 // band) * LANES) & (ring - 1)
                masks.append(jnp.where(offset < count, 1.0, 0.0))
        mask = jnp.concatenate(masks, axis=0).astype(jnp.bfloat16)

        def tables(modes):
            lane_modes = jnp.concatenate([modes] * 4, axis=1)
            width = 4 * chunk
            kind = iota((1, width), 1) // chunk
            cosine, sine = circle(iota((LANES, width), 0) * lane_modes, ring)
            table = jnp.where(kind % 2 == 0, cosine, sine)
            high = table.astype(jnp.bfloat16)
            low = (table - high.astype(jnp.float32)).astype(jnp.bfloat16)
            pixel = first_pixel + (iota((pieces * band, width), 0) // band) * LANES
            cosine, sine = circle(pixel * lane_modes, ring)
            turn = jnp.where(kind == 0, cosine, jnp.where(kind == 3, -cosine, -sine))
            return jnp.concatenate([high, low], axis=0), turn

        def sums(values, table, turn):
            wide = jnp.concatenate([values, values], axis=1)
            product = jnp.dot(wide, table, preferred_element_type=jnp.float32)
            parts = []
            for h in range(2):
                total = None
                for t in range(pieces * band // 8):
                    at = h * pieces * band + t * 8
                    term = product[at : at + 8] * turn[t * 8 : t * 8 + 8]
                    total = term if total is None else total + term
                folded = total[:band]
                for k in range(band, 8, band):
                    folded = folded + total[k : k + band]
                parts.append(folded)
            return jnp.concatenate(parts, axis=0)

        def send(gathered, owners, index):
            turned = gathered.T
            real = turned[:chunk] + turned[chunk : 2 * chunk]
            imag = turned[2 * chunk : 3 * chunk] + turned[3 * chunk :]
            both = jnp.concatenate([real, imag], axis=1)
            for o in range(owners):
                for c in range(copies):
                    out_ref[index * owners * copies + o * copies + c] = both[o * owned : (o + 1) * owned]

        owners = chunk // owned
        if chunks == 1:
            table, turn = tables(modes_ref[0])
            found = []
            for x in range(maps):
                sky_copies[x].wait()
                found.append(sums(sky_ref[pl.ds(x * rows, rows)] * mask, table, turn))
            send(jnp.concatenate(found, axis=0), owners, 0)
        else:
            for x in range(maps):
                sky_copies[x].wait()
                sky_ref[pl.ds(x * rows, rows)] = sky_ref[pl.ds(x * rows, rows)] * mask

            def step(index, carry):
                table, turn = tables(modes_ref[index])
                found = [sums(sky_ref[pl.ds(x * rows, rows)], table, turn) for x in range(maps)]
                send(jnp.concatenate(found, axis=0), owners, index)
                return carry

            lax.fori_loop(0, chunks, step, 0)

    return body


def legendre_kernel(maps, band, owned, blocks, copies, degrees, ring):
    scale = DIFFUSION / math.sqrt(ring)
    cycles = blocks * band

    def body(sums_ref, aux_ref, legendre_ref, out_ref):
        lane = iota((1, LANES), 1)
        cycle = lane % band
        south = (lane // band) % 2 == 1
        parts = []
        for b in range(blocks):
            total = sums_ref[b * copies]
            for c in range(1, copies):
                total = total + sums_ref[b * copies + c]
            parts.append(total)
        here = jnp.concatenate(parts, axis=0)
        rows = blocks * owned
        none = jnp.zeros((owned, LANES), jnp.float32)
        prior = jnp.concatenate([none, here[:-owned]], axis=0)
        later = jnp.concatenate([here[owned:], none], axis=0)

        def moved(value, shift):
            return pltpu.roll(value, shift % LANES, 1)

        above = jnp.where(cycle == 0, moved(prior, 1 - band), moved(here, 1))
        other = jnp.where(south, moved(here, band), moved(here, -band))
        is_last = iota((rows, 1), 0) >= rows - owned
        edge = jnp.where(is_last, other, moved(later, band - 1))
        below = jnp.where(cycle == band - 1, edge, moved(here, -1))

        def wide(value):
            return jnp.concatenate([value] * (rows // 8), axis=0)

        smooth = wide(aux_ref[0]) * here + scale * (above + below)
        turned = smooth * wide(aux_ref[1]) + moved(smooth, LANES // 2) * wide(aux_ref[2])
        folded = jnp.where(south, moved(turned, band) - turned, turned + moved(turned, -band))
        folded = folded.astype(jnp.bfloat16)

        depth = owned * cycles
        row = iota((rows, depth), 0)
        column = iota((rows, depth), 1)
        spread = (row // owned == (column // band) % blocks) & (row % owned == column // cycles)
        spread = jnp.where(spread, 1.0, 0.0).astype(jnp.bfloat16)
        across = lax.dot_general(
            folded, spread, (((0,), (0,)), ((), ())), preferred_element_type=jnp.float32
        )
        match = iota((LANES, depth), 0) % band == iota((LANES, depth), 1) % band
        across = jnp.where(match, across, 0.0).astype(jnp.bfloat16)
        height = 2 * maps * 2 * owned
        row = iota((height, LANES), 0)
        column = iota((height, LANES), 1)
        fold, x, part = row // (maps * 2 * owned), (row // (2 * owned)) % maps, (row // owned) % 2
        pick = column // band == part * (maps * 2) + x * 2 + fold
        pick = jnp.where(pick, 1.0, 0.0).astype(jnp.bfloat16)
        weights = jnp.dot(pick, across, preferred_element_type=jnp.float32)
        match = iota((height, depth), 0) % owned == iota((height, depth), 1) // cycles
        weights = jnp.where(match, weights, 0.0).astype(jnp.bfloat16)

        sums = jnp.dot(weights, legendre_ref[...], preferred_element_type=jnp.float32)
        mode = aux_ref[3].astype(jnp.int32)
        half = height // 2
        group = 8 // owned
        columns = degrees // LANES
        first = lax.axis_index("lblk") * degrees
        picked = []
        for j in range(columns):
            degree = first + j * LANES + iota((8, LANES), 1)
            even = ((degree + mode) & 1) == 0
            inside = degree >= mode
            line = []
            for i in range(half // 8):
                plus = sums[i * 8 : i * 8 + 8, j * LANES : (j + 1) * LANES]
                minus = sums[half + i * 8 : half + i * 8 + 8, j * LANES : (j + 1) * LANES]
                line.append(jnp.where(inside, jnp.where(even, plus, minus), 0.0))
            picked.append(line)
        for i in range(half // 8):
            for g in range(group):
                for j in range(columns):
                    at = ((i * group + g) * columns + j) * owned
                    out_ref[at : at + owned] = picked[j][i][g * owned : (g + 1) * owned]

    return body


def local(sky, arc_start, arc_count, owner_modes, legendre):
    maps, _, band, quarter = sky.shape
    slots = owner_modes.shape[0]
    owned, groups, _, degrees = legendre.shape
    blocks, copies = lax.axis_size("blk"), lax.axis_size("lblk")
    ring = quarter * copies
    chunk = min(slots, LANES // 4)
    chunks = slots // chunk
    pieces = quarter // LANES
    sky_rows = sky.reshape(maps, 2, band, pieces, LANES).transpose(0, 1, 3, 2, 4)
    sky_rows = sky_rows.reshape(maps * 2 * pieces * band, LANES)
    anywhere = pl.BlockSpec(memory_space=pl.ANY)
    whole = pl.BlockSpec(memory_space=pltpu.VMEM)
    partial, aux = pl.pallas_call(
        fourier_kernel(maps, band, quarter, ring, owned, copies, chunk, chunks),
        out_shape=(
            jax.ShapeDtypeStruct((blocks * copies, owned, LANES), jnp.float32),
            jax.ShapeDtypeStruct((4, 8, LANES), jnp.float32),
        ),
        in_specs=[anywhere] * 5,
        out_specs=(whole, whole),
        scratch_shapes=[
            pltpu.VMEM(sky_rows.shape, jnp.bfloat16),
            pltpu.SMEM(arc_start.shape, jnp.int32),
            pltpu.SMEM(arc_count.shape, jnp.int32),
            pltpu.VMEM((chunks, 1, chunk), jnp.int32),
            pltpu.SMEM((slots,), jnp.int32),
            pltpu.SemaphoreType.DMA((4,)),
            pltpu.SemaphoreType.DMA((maps,)),
        ],
        name="fourier",
    )(sky_rows, arc_start, arc_count, owner_modes.reshape(chunks, 1, chunk), owner_modes)
    received = lax.all_to_all(partial, ("blk", "lblk"), split_axis=0, concat_axis=0, tiled=True)
    columns = degrees // LANES
    result = pl.pallas_call(
        legendre_kernel(maps, band, owned, blocks, copies, degrees, ring),
        out_shape=jax.ShapeDtypeStruct((maps * 2 * columns * owned, LANES), jnp.float32),
        in_specs=[whole] * 3,
        out_specs=whole,
        name="legendre",
    )(received, aux, legendre.reshape(owned * groups * band, degrees))
    result = result.reshape(maps, 2, columns, owned, LANES).transpose(0, 1, 3, 2, 4)
    return result.reshape(maps, 2, owned, degrees)


def solution(mesh):
    return jax.shard_map(
        local,
        mesh=mesh,
        in_specs=(
            P(None, None, "blk", "lblk"),
            P(None, "blk"),
            P(None, "blk"),
            P(),
            P("blk", None, None, "lblk"),
        ),
        out_specs=P(None, None, "blk", "lblk"),
        check_vma=False,
    )
```

```python
import math

import jax
import jax.numpy as jnp
from jax import lax
from jax.experimental import pallas as pl
from jax.experimental.pallas import tpu as pltpu
from jax.sharding import PartitionSpec as P

DIFFUSION = 0.2
LANES = 128
STEP = 4
ROOM = pltpu.CompilerParams(vmem_limit_bytes=28 * 2**20)

COS_TERMS = (1.0, -1.0 / 2, 1.0 / 24, -1.0 / 720, 1.0 / 40320, -1.0 / 3628800)
SIN_TERMS = (1.0, -1.0 / 6, 1.0 / 120, -1.0 / 5040, 1.0 / 362880)


def horner(terms, square):
    total = jnp.full_like(square, terms[-1])
    for term in terms[-2::-1]:
        total = total * square + term
    return total


def circle(index, turn):
    index = index & (turn - 1)
    quadrant = (index * 4 + turn // 2) >> (turn.bit_length() - 1)
    rest = (index - quadrant * (turn // 4)).astype(jnp.float32) * (2.0 * math.pi / turn)
    square = rest * rest
    cosine = horner(COS_TERMS, square)
    sine = rest * horner(SIN_TERMS, square)
    odd = (quadrant & 1) == 1
    swapped_cos = jnp.where(odd, sine, cosine)
    swapped_sin = jnp.where(odd, cosine, sine)
    cos_sign = ((quadrant + 1) & 2) == 2
    sin_sign = (quadrant & 2) == 2
    return (
        jnp.where(cos_sign, -swapped_cos, swapped_cos),
        jnp.where(sin_sign, -swapped_sin, swapped_sin),
    )


def iota(shape, axis):
    return lax.broadcasted_iota(jnp.int32, shape, axis)


def table_kernel(band, quarter, ring, owned, chunk):
    pieces = quarter // LANES
    width = 4 * chunk

    def body(start_ref, count_ref, modes_ref, mask_ref, table_ref, turn_ref, aux_ref):
        first_pixel = lax.axis_index("lblk") * quarter
        block = lax.axis_index("blk")
        row = iota((8, LANES), 0)
        lane = iota((8, LANES), 1)
        mine = jnp.zeros((8, LANES), jnp.int32)
        for s in range(owned):
            mine = jnp.where(row % owned == s, modes_ref[block * owned + s], mine)
        step_cos, _ = circle(mine, ring)
        turn_cos, turn_sin = circle(mine * (lane % band % 2), 2 * ring)
        aux_ref[0] = DIFFUSION / math.sqrt(ring) * (1.0 + 2.0 * step_cos)
        aux_ref[1] = turn_cos
        aux_ref[2] = jnp.where(lane < LANES // 2, turn_sin, -turn_sin)
        aux_ref[3] = mine.astype(jnp.float32)

        masks = []
        for h in range(2):
            start = jnp.zeros((8, LANES), jnp.int32)
            count = jnp.zeros((8, LANES), jnp.int32)
            for k in range(band):
                start = jnp.where(row % band == k, start_ref[h, k], start)
                count = jnp.where(row % band == k, count_ref[h, k], count)
            shifted = first_pixel + (row // band) * LANES + lane - start
            for t in range(pieces * band // 8):
                offset = (shifted + t * (8 // band) * LANES) & (ring - 1)
                masks.append(jnp.where(offset < count, 1.0, 0.0))
        mask_ref[...] = jnp.concatenate(masks, axis=0).astype(jnp.bfloat16)

        kind = iota((1, width), 1) // chunk
        column = iota((1, width), 1) % chunk
        for g in range(modes_ref.shape[0] // chunk):
            modes = jnp.zeros((1, width), jnp.int32)
            for s in range(chunk):
                modes = jnp.where(column == s, modes_ref[g * chunk + s], modes)
            cosine, sine = circle(iota((LANES, width), 0) * modes, ring)
            table = jnp.where(kind % 2 == 0, cosine, sine)
            high = table.astype(jnp.bfloat16)
            table_ref[g, :LANES] = high
            table_ref[g, LANES:] = (table - high.astype(jnp.float32)).astype(jnp.bfloat16)
            pixel = first_pixel + (iota((pieces * band, width), 0) // band) * LANES
            cosine, sine = circle(pixel * modes, ring)
            turn_ref[g] = jnp.where(kind == 0, cosine, jnp.where(kind == 3, -cosine, -sine))

    return body


def fourier_kernel(maps, band, pieces, owned, copies, chunk, chunks, step):
    rows = 2 * pieces * band
    owners = chunk // owned

    def body(sky_ref, mask_ref, table_ref, turn_ref, out_ref):
        def run(g):
            found = []
            for x in range(0, maps, step):
                values = [sky_ref[(x + i) * rows : (x + i + 1) * rows] * mask_ref[...] for i in range(step)]
                values = jnp.concatenate(values, axis=0)
                wide = jnp.concatenate([values, values], axis=1)
                product = jnp.dot(wide, table_ref[g], preferred_element_type=jnp.float32)
                for h in range(2 * step):
                    total = None
                    for t in range(pieces * band // 8):
                        at = h * pieces * band + t * 8
                        term = product[at : at + 8] * turn_ref[g, t * 8 : t * 8 + 8]
                        total = term if total is None else total + term
                    folded = total[:band]
                    for k in range(band, 8, band):
                        folded = folded + total[k : k + band]
                    found.append(folded)
            turned = jnp.concatenate(found, axis=0).T
            real = turned[:chunk] + turned[chunk : 2 * chunk]
            imag = turned[2 * chunk : 3 * chunk] + turned[3 * chunk :]
            both = jnp.concatenate([real, imag], axis=1)
            for o in range(owners):
                for c in range(copies):
                    out_ref[(g * owners + o) * copies + c] = both[o * owned : (o + 1) * owned]

        if chunks == 1:
            run(0)
        else:
            lax.fori_loop(0, chunks, lambda g, _: run(g), None)

    return body


def legendre_kernel(maps, band, owned, blocks, copies, degrees, ring):
    scale = DIFFUSION / math.sqrt(ring)
    cycles = blocks * band

    def body(sums_ref, aux_ref, legendre_ref, out_ref):
        lane = iota((1, LANES), 1)
        cycle = lane % band
        south = (lane // band) % 2 == 1
        parts = []
        for b in range(blocks):
            total = sums_ref[b * copies]
            for c in range(1, copies):
                total = total + sums_ref[b * copies + c]
            parts.append(total)
        here = jnp.concatenate(parts, axis=0)
        rows = blocks * owned
        none = jnp.zeros((owned, LANES), jnp.float32)
        prior = jnp.concatenate([none, here[:-owned]], axis=0)
        later = jnp.concatenate([here[owned:], none], axis=0)

        def moved(value, shift):
            return pltpu.roll(value, shift % LANES, 1)

        above = jnp.where(cycle == 0, moved(prior, 1 - band), moved(here, 1))
        other = jnp.where(south, moved(here, band), moved(here, -band))
        is_last = iota((rows, 1), 0) >= rows - owned
        edge = jnp.where(is_last, other, moved(later, band - 1))
        below = jnp.where(cycle == band - 1, edge, moved(here, -1))

        def wide(value):
            return jnp.concatenate([value] * (rows // 8), axis=0)

        smooth = wide(aux_ref[0]) * here + scale * (above + below)
        turned = smooth * wide(aux_ref[1]) + moved(smooth, LANES // 2) * wide(aux_ref[2])
        folded = jnp.where(south, moved(turned, band) - turned, turned + moved(turned, -band))
        folded = folded.astype(jnp.bfloat16)

        depth = owned * cycles
        row = iota((rows, depth), 0)
        column = iota((rows, depth), 1)
        spread = (row // owned == (column // band) % blocks) & (row % owned == column // cycles)
        spread = jnp.where(spread, 1.0, 0.0).astype(jnp.bfloat16)
        across = lax.dot_general(
            folded, spread, (((0,), (0,)), ((), ())), preferred_element_type=jnp.float32
        )
        match = iota((LANES, depth), 0) % band == iota((LANES, depth), 1) % band
        across = jnp.where(match, across, 0.0).astype(jnp.bfloat16)
        height = 2 * maps * 2 * owned
        row = iota((height, LANES), 0)
        column = iota((height, LANES), 1)
        fold, x, part = row // (maps * 2 * owned), (row // (2 * owned)) % maps, (row // owned) % 2
        pick = column // band == part * (maps * 2) + x * 2 + fold
        pick = jnp.where(pick, 1.0, 0.0).astype(jnp.bfloat16)
        weights = jnp.dot(pick, across, preferred_element_type=jnp.float32)
        match = iota((height, depth), 0) % owned == iota((height, depth), 1) // cycles
        weights = jnp.where(match, weights, 0.0).astype(jnp.bfloat16)

        sums = jnp.dot(weights, legendre_ref[...], preferred_element_type=jnp.float32)
        mode = aux_ref[3].astype(jnp.int32)
        half = height // 2
        group = 8 // owned
        columns = degrees // LANES
        first = lax.axis_index("lblk") * degrees
        picked = []
        for j in range(columns):
            degree = first + j * LANES + iota((8, LANES), 1)
            even = ((degree + mode) & 1) == 0
            inside = degree >= mode
            line = []
            for i in range(half // 8):
                plus = sums[i * 8 : i * 8 + 8, j * LANES : (j + 1) * LANES]
                minus = sums[half + i * 8 : half + i * 8 + 8, j * LANES : (j + 1) * LANES]
                line.append(jnp.where(inside, jnp.where(even, plus, minus), 0.0))
            picked.append(line)
        for i in range(half // 8):
            for g in range(group):
                for j in range(columns):
                    at = ((i * group + g) * columns + j) * owned
                    out_ref[at : at + owned] = picked[j][i][g * owned : (g + 1) * owned]

    return body


def on_chip(value):
    return pltpu.with_memory_space_constraint(value, pltpu.VMEM)


def local(sky, arc_start, arc_count, owner_modes, legendre):
    maps, _, band, quarter = sky.shape
    slots = owner_modes.shape[0]
    owned, groups, _, degrees = legendre.shape
    blocks, copies = lax.axis_size("blk"), lax.axis_size("lblk")
    ring = quarter * copies
    chunk = min(slots, LANES // 4)
    chunks = slots // chunk
    pieces = quarter // LANES
    sky_rows = sky.reshape(maps, 2, band, pieces, LANES).transpose(0, 1, 3, 2, 4)
    sky_rows = sky_rows.reshape(maps * 2 * pieces * band, LANES)
    scalars = pl.BlockSpec(memory_space=pltpu.SMEM)
    whole = pl.BlockSpec(memory_space=pltpu.VMEM)
    mask, table, turn, aux = pl.pallas_call(
        table_kernel(band, quarter, ring, owned, chunk),
        out_shape=(
            pltpu.VMEM((2 * pieces * band, LANES), jnp.bfloat16),
            pltpu.VMEM((chunks, 2 * LANES, 4 * chunk), jnp.bfloat16),
            pltpu.VMEM((chunks, pieces * band, 4 * chunk), jnp.float32),
            pltpu.VMEM((4, 8, LANES), jnp.float32),
        ),
        in_specs=[scalars] * 3,
        out_specs=(whole,) * 4,
        cost_estimate=pl.CostEstimate(flops=10**9, bytes_accessed=4 * 10**6, transcendentals=10**6),
        compiler_params=ROOM,
        name="tables",
    )(arc_start, arc_count, owner_modes)
    partial = pl.pallas_call(
        fourier_kernel(maps, band, pieces, owned, copies, chunk, chunks, STEP),
        out_shape=pltpu.VMEM((blocks * copies, owned, LANES), jnp.float32),
        in_specs=[whole] * 4,
        out_specs=whole,
        compiler_params=ROOM,
        name="fourier",
    )(*(on_chip(v) for v in (sky_rows, mask, table, turn)))
    received = lax.all_to_all(partial, ("blk", "lblk"), split_axis=0, concat_axis=0, tiled=True)
    columns = degrees // LANES
    result = pl.pallas_call(
        legendre_kernel(maps, band, owned, blocks, copies, degrees, ring),
        out_shape=jax.ShapeDtypeStruct((maps * 2 * columns * owned, LANES), jnp.float32),
        in_specs=[whole] * 3,
        out_specs=whole,
        compiler_params=ROOM,
        name="legendre",
    )(on_chip(received), on_chip(aux), on_chip(legendre.reshape(owned * groups * band, degrees)))
    result = result.reshape(maps, 2, columns, owned, LANES).transpose(0, 1, 3, 2, 4)
    return result.reshape(maps, 2, owned, degrees)


def solution(mesh):
    return jax.shard_map(
        local,
        mesh=mesh,
        in_specs=(
            P(None, None, "blk", "lblk"),
            P(None, "blk"),
            P(None, "blk"),
            P(),
            P("blk", None, None, "lblk"),
        ),
        out_specs=P(None, None, "blk", "lblk"),
        check_vma=False,
    )
```

```python
import math

import jax
import jax.numpy as jnp
from jax import lax
from jax.experimental import pallas as pl
from jax.experimental.pallas import tpu as pltpu
from jax.sharding import PartitionSpec as P

DIFFUSION = 0.2
LANES = 128
STEP = 4

COS_TERMS = (1.0, -1.0 / 2, 1.0 / 24, -1.0 / 720, 1.0 / 40320, -1.0 / 3628800)
SIN_TERMS = (1.0, -1.0 / 6, 1.0 / 120, -1.0 / 5040, 1.0 / 362880)


def horner(terms, square):
    total = jnp.full_like(square, terms[-1])
    for term in terms[-2::-1]:
        total = total * square + term
    return total


def circle(index, turn):
    index = index & (turn - 1)
    quadrant = (index * 4 + turn // 2) >> (turn.bit_length() - 1)
    rest = (index - quadrant * (turn // 4)).astype(jnp.float32) * (2.0 * math.pi / turn)
    square = rest * rest
    cosine = horner(COS_TERMS, square)
    sine = rest * horner(SIN_TERMS, square)
    odd = (quadrant & 1) == 1
    swapped_cos = jnp.where(odd, sine, cosine)
    swapped_sin = jnp.where(odd, cosine, sine)
    cos_sign = ((quadrant + 1) & 2) == 2
    sin_sign = (quadrant & 2) == 2
    return (
        jnp.where(cos_sign, -swapped_cos, swapped_cos),
        jnp.where(sin_sign, -swapped_sin, swapped_sin),
    )


def iota(shape, axis):
    return lax.broadcasted_iota(jnp.int32, shape, axis)


def table_kernel(band, quarter, ring, owned, chunk):
    pieces = quarter // LANES
    width = 4 * chunk

    def body(start_ref, count_ref, modes_ref, mask_ref, table_ref, turn_ref, aux_ref):
        first_pixel = lax.axis_index("lblk") * quarter
        block = lax.axis_index("blk")
        row = iota((8, LANES), 0)
        lane = iota((8, LANES), 1)
        mine = jnp.zeros((8, LANES), jnp.int32)
        for s in range(owned):
            mine = jnp.where(row % owned == s, modes_ref[block * owned + s], mine)
        step_cos, _ = circle(mine, ring)
        turn_cos, turn_sin = circle(mine * (lane % band % 2), 2 * ring)
        aux_ref[0] = DIFFUSION / math.sqrt(ring) * (1.0 + 2.0 * step_cos)
        aux_ref[1] = turn_cos
        aux_ref[2] = jnp.where(lane < LANES // 2, turn_sin, -turn_sin)
        aux_ref[3] = mine.astype(jnp.float32)

        masks = []
        for h in range(2):
            start = jnp.zeros((8, LANES), jnp.int32)
            count = jnp.zeros((8, LANES), jnp.int32)
            for k in range(band):
                start = jnp.where(row % band == k, start_ref[h, k], start)
                count = jnp.where(row % band == k, count_ref[h, k], count)
            shifted = first_pixel + (row // band) * LANES + lane - start
            for t in range(pieces * band // 8):
                offset = (shifted + t * (8 // band) * LANES) & (ring - 1)
                masks.append(jnp.where(offset < count, 1.0, 0.0))
        mask_ref[...] = jnp.concatenate(masks, axis=0).astype(jnp.bfloat16)

        kind = iota((1, width), 1) // chunk
        column = iota((1, width), 1) % chunk
        for g in range(modes_ref.shape[0] // chunk):
            modes = jnp.zeros((1, width), jnp.int32)
            for s in range(chunk):
                modes = jnp.where(column == s, modes_ref[g * chunk + s], modes)
            cosine, sine = circle(iota((LANES, width), 0) * modes, ring)
            table = jnp.where(kind % 2 == 0, cosine, sine)
            high = table.astype(jnp.bfloat16)
            table_ref[g, :LANES] = high
            table_ref[g, LANES:] = (table - high.astype(jnp.float32)).astype(jnp.bfloat16)
            pixel = first_pixel + (iota((pieces * band, width), 0) // band) * LANES
            cosine, sine = circle(pixel * modes, ring)
            turn_ref[g] = jnp.where(kind == 0, cosine, jnp.where(kind == 3, -cosine, -sine))

    return body


def fourier_kernel(maps, band, pieces, owned, copies, chunk, chunks, step):
    rows = 2 * pieces * band
    owners = chunk // owned

    def body(sky_ref, mask_ref, table_ref, turn_ref, out_ref):
        def run(g):
            found = []
            for x in range(0, maps, step):
                values = [sky_ref[(x + i) * rows : (x + i + 1) * rows] * mask_ref[...] for i in range(step)]
                values = jnp.concatenate(values, axis=0)
                wide = jnp.concatenate([values, values], axis=1)
                product = jnp.dot(wide, table_ref[g], preferred_element_type=jnp.float32)
                for h in range(2 * step):
                    total = None
                    for t in range(pieces * band // 8):
                        at = h * pieces * band + t * 8
                        term = product[at : at + 8] * turn_ref[g, t * 8 : t * 8 + 8]
                        total = term if total is None else total + term
                    folded = total[:band]
                    for k in range(band, 8, band):
                        folded = folded + total[k : k + band]
                    found.append(folded)
            turned = jnp.concatenate(found, axis=0).T
            real = turned[:chunk] + turned[chunk : 2 * chunk]
            imag = turned[2 * chunk : 3 * chunk] + turned[3 * chunk :]
            both = jnp.concatenate([real, imag], axis=1)
            for o in range(owners):
                for c in range(copies):
                    out_ref[(g * owners + o) * copies + c] = both[o * owned : (o + 1) * owned]

        if chunks == 1:
            run(0)
        else:
            lax.fori_loop(0, chunks, lambda g, _: run(g), None)

    return body


def legendre_kernel(maps, band, owned, blocks, copies, degrees, ring):
    scale = DIFFUSION / math.sqrt(ring)
    cycles = blocks * band

    def body(sums_ref, aux_ref, legendre_ref, out_ref):
        lane = iota((1, LANES), 1)
        cycle = lane % band
        south = (lane // band) % 2 == 1
        parts = []
        for b in range(blocks):
            total = sums_ref[b * copies]
            for c in range(1, copies):
                total = total + sums_ref[b * copies + c]
            parts.append(total)
        here = jnp.concatenate(parts, axis=0)
        rows = blocks * owned
        none = jnp.zeros((owned, LANES), jnp.float32)
        prior = jnp.concatenate([none, here[:-owned]], axis=0)
        later = jnp.concatenate([here[owned:], none], axis=0)

        def moved(value, shift):
            return pltpu.roll(value, shift % LANES, 1)

        above = jnp.where(cycle == 0, moved(prior, 1 - band), moved(here, 1))
        other = jnp.where(south, moved(here, band), moved(here, -band))
        is_last = iota((rows, 1), 0) >= rows - owned
        edge = jnp.where(is_last, other, moved(later, band - 1))
        below = jnp.where(cycle == band - 1, edge, moved(here, -1))

        def wide(value):
            return jnp.concatenate([value] * (rows // 8), axis=0)

        smooth = wide(aux_ref[0]) * here + scale * (above + below)
        turned = smooth * wide(aux_ref[1]) + moved(smooth, LANES // 2) * wide(aux_ref[2])
        folded = jnp.where(south, moved(turned, band) - turned, turned + moved(turned, -band))
        folded = folded.astype(jnp.bfloat16)

        depth = owned * cycles
        row = iota((rows, depth), 0)
        column = iota((rows, depth), 1)
        spread = (row // owned == (column // band) % blocks) & (row % owned == column // cycles)
        spread = jnp.where(spread, 1.0, 0.0).astype(jnp.bfloat16)
        across = lax.dot_general(
            folded, spread, (((0,), (0,)), ((), ())), preferred_element_type=jnp.float32
        )
        match = iota((LANES, depth), 0) % band == iota((LANES, depth), 1) % band
        across = jnp.where(match, across, 0.0).astype(jnp.bfloat16)
        height = 2 * maps * 2 * owned
        row = iota((height, LANES), 0)
        column = iota((height, LANES), 1)
        fold, x, part = row // (maps * 2 * owned), (row // (2 * owned)) % maps, (row // owned) % 2
        pick = column // band == part * (maps * 2) + x * 2 + fold
        pick = jnp.where(pick, 1.0, 0.0).astype(jnp.bfloat16)
        weights = jnp.dot(pick, across, preferred_element_type=jnp.float32)
        match = iota((height, depth), 0) % owned == iota((height, depth), 1) // cycles
        weights = jnp.where(match, weights, 0.0).astype(jnp.bfloat16)

        sums = jnp.dot(weights, legendre_ref[...], preferred_element_type=jnp.float32)
        mode = aux_ref[3].astype(jnp.int32)
        half = height // 2
        group = 8 // owned
        columns = degrees // LANES
        first = lax.axis_index("lblk") * degrees
        picked = []
        for j in range(columns):
            degree = first + j * LANES + iota((8, LANES), 1)
            even = ((degree + mode) & 1) == 0
            inside = degree >= mode
            line = []
            for i in range(half // 8):
                plus = sums[i * 8 : i * 8 + 8, j * LANES : (j + 1) * LANES]
                minus = sums[half + i * 8 : half + i * 8 + 8, j * LANES : (j + 1) * LANES]
                line.append(jnp.where(inside, jnp.where(even, plus, minus), 0.0))
            picked.append(line)
        for i in range(half // 8):
            for g in range(group):
                for j in range(columns):
                    at = ((i * group + g) * columns + j) * owned
                    out_ref[at : at + owned] = picked[j][i][g * owned : (g + 1) * owned]

    return body


def on_chip(value):
    return pltpu.with_memory_space_constraint(value, pltpu.VMEM)


def local(sky, arc_start, arc_count, owner_modes, legendre):
    maps, _, band, quarter = sky.shape
    slots = owner_modes.shape[0]
    owned, groups, _, degrees = legendre.shape
    blocks, copies = lax.axis_size("blk"), lax.axis_size("lblk")
    ring = quarter * copies
    chunk = min(slots, LANES // 4)
    chunks = slots // chunk
    room = pltpu.CompilerParams(vmem_limit_bytes=28 * 2**20 if chunks > 1 else None)
    pieces = quarter // LANES
    sky_rows = sky.reshape(maps, 2, band, pieces, LANES).transpose(0, 1, 3, 2, 4)
    sky_rows = sky_rows.reshape(maps * 2 * pieces * band, LANES)
    scalars = pl.BlockSpec(memory_space=pltpu.SMEM)
    whole = pl.BlockSpec(memory_space=pltpu.VMEM)
    mask, table, turn, aux = pl.pallas_call(
        table_kernel(band, quarter, ring, owned, chunk),
        out_shape=(
            pltpu.VMEM((2 * pieces * band, LANES), jnp.bfloat16),
            pltpu.VMEM((chunks, 2 * LANES, 4 * chunk), jnp.bfloat16),
            pltpu.VMEM((chunks, pieces * band, 4 * chunk), jnp.float32),
            pltpu.VMEM((4, 8, LANES), jnp.float32),
        ),
        in_specs=[scalars] * 3,
        out_specs=(whole,) * 4,
        cost_estimate=pl.CostEstimate(flops=10**9, bytes_accessed=4 * 10**6, transcendentals=10**6),
        compiler_params=room,
        name="tables",
    )(arc_start, arc_count, owner_modes)
    partial = pl.pallas_call(
        fourier_kernel(maps, band, pieces, owned, copies, chunk, chunks, STEP),
        out_shape=pltpu.VMEM((blocks * copies, owned, LANES), jnp.float32),
        in_specs=[whole] * 4,
        out_specs=whole,
        compiler_params=room,
        name="fourier",
    )(*(on_chip(v) for v in (sky_rows, mask, table, turn)))
    received = lax.all_to_all(partial, ("blk", "lblk"), split_axis=0, concat_axis=0, tiled=True)
    legendre, received = lax.optimization_barrier((legendre, received))
    legendre_rows = legendre.reshape(owned * groups * band, degrees)
    columns = degrees // LANES
    result = pl.pallas_call(
        legendre_kernel(maps, band, owned, blocks, copies, degrees, ring),
        out_shape=jax.ShapeDtypeStruct((maps * 2 * columns * owned, LANES), jnp.float32),
        in_specs=[whole] * 3,
        out_specs=whole,
        compiler_params=room,
        name="legendre",
    )(on_chip(received), on_chip(aux), on_chip(legendre_rows))
    result = result.reshape(maps, 2, columns, owned, LANES).transpose(0, 1, 3, 2, 4)
    return result.reshape(maps, 2, owned, degrees)


def solution(mesh):
    return jax.shard_map(
        local,
        mesh=mesh,
        in_specs=(
            P(None, None, "blk", "lblk"),
            P(None, "blk"),
            P(None, "blk"),
            P(),
            P("blk", None, None, "lblk"),
        ),
        out_specs=P(None, None, "blk", "lblk"),
        check_vma=False,
    )
```

```python
import math

import jax
import jax.numpy as jnp
from jax import lax
from jax.experimental import pallas as pl
from jax.experimental.pallas import tpu as pltpu
from jax.sharding import PartitionSpec as P

DIFFUSION = 0.2
LANES = 128
STEP = 4

COS_TERMS = (1.0, -1.0 / 2, 1.0 / 24, -1.0 / 720, 1.0 / 40320, -1.0 / 3628800)
SIN_TERMS = (1.0, -1.0 / 6, 1.0 / 120, -1.0 / 5040, 1.0 / 362880)


def horner(terms, square):
    total = jnp.full_like(square, terms[-1])
    for term in terms[-2::-1]:
        total = total * square + term
    return total


def circle(index, turn):
    index = index & (turn - 1)
    quadrant = (index * 4 + turn // 2) >> (turn.bit_length() - 1)
    rest = (index - quadrant * (turn // 4)).astype(jnp.float32) * (2.0 * math.pi / turn)
    square = rest * rest
    cosine = horner(COS_TERMS, square)
    sine = rest * horner(SIN_TERMS, square)
    odd = (quadrant & 1) == 1
    swapped_cos = jnp.where(odd, sine, cosine)
    swapped_sin = jnp.where(odd, cosine, sine)
    cos_sign = ((quadrant + 1) & 2) == 2
    sin_sign = (quadrant & 2) == 2
    return (
        jnp.where(cos_sign, -swapped_cos, swapped_cos),
        jnp.where(sin_sign, -swapped_sin, swapped_sin),
    )


def iota(shape, axis):
    return lax.broadcasted_iota(jnp.int32, shape, axis)


def powers(first, count):
    return [first << i for i in range(count.bit_length() - 1)]


def rotations(index, lane_modes, ring):
    amount = jnp.zeros((len(index), 1), jnp.int32)
    for i, value in enumerate(index):
        amount = jnp.where(iota(amount.shape, 0) == i, value, amount)
    return circle(amount * lane_modes, ring)


def unrolled(first, second, cosines, sines):
    blocks = [(first, second)]
    for i in range(cosines.shape[0]):
        cosine, sine = cosines[i : i + 1], sines[i : i + 1]
        blocks += [(f * cosine - s * sine, s * cosine + f * sine) for f, s in blocks]
    return [f for f, _ in blocks]


def table_kernel(band, quarter, ring, owned, chunk):
    pieces = quarter // LANES
    width = 4 * chunk

    def body(start_ref, count_ref, modes_ref, lane_modes_ref, mask_ref, table_ref, turn_ref, aux_ref):
        first_pixel = lax.axis_index("lblk") * quarter
        block = lax.axis_index("blk")
        row = iota((8, LANES), 0)
        lane = iota((8, LANES), 1)
        mine = jnp.zeros((8, LANES), jnp.int32)
        for s in range(owned):
            mine = jnp.where(row % owned == s, modes_ref[block * owned + s], mine)
        half = LANES // 2
        odd = (lane // (half // band)) % band % 2
        scale = DIFFUSION / math.sqrt(ring)
        step_cos, _ = circle(mine, ring)
        turn_cos, turn_sin = circle(mine * odd, 2 * ring)
        turn_sin = jnp.where(lane < half, turn_sin, -turn_sin)
        centre = scale * (1.0 + 2.0 * step_cos)
        aux_ref[0] = turn_cos * centre
        aux_ref[1] = turn_cos * scale
        aux_ref[2] = turn_sin * centre
        aux_ref[3] = turn_sin * scale
        aux_ref[4] = mine.astype(jnp.float32)

        masks = []
        for h in range(2):
            start = jnp.zeros((8, LANES), jnp.int32)
            count = jnp.zeros((8, LANES), jnp.int32)
            for k in range(band):
                start = jnp.where(row % band == k, start_ref[h, k], start)
                count = jnp.where(row % band == k, count_ref[h, k], count)
            shifted = first_pixel + (row // band) * LANES + lane - start
            for t in range(pieces * band // 8):
                offset = (shifted + t * (8 // band) * LANES) & (ring - 1)
                masks.append(jnp.where(offset < count, 1.0, 0.0))
        mask_ref[...] = jnp.concatenate(masks, axis=0).astype(jnp.bfloat16)

        kind = iota((1, width), 1) // chunk
        step = 8 // band * LANES
        in_table = powers(8, LANES // 8)
        in_turn = powers(step, quarter // step)
        for g in range(lane_modes_ref.shape[0]):
            modes = jnp.concatenate([lane_modes_ref[g]] * 4, axis=1)
            cosines, sines = rotations(in_table + in_turn, modes, ring)
            cosine, sine = circle(iota((8, width), 0) * modes, ring)
            is_cos = kind % 2 == 0
            blocks = unrolled(
                jnp.where(is_cos, cosine, sine),
                jnp.where(is_cos, sine, -cosine),
                cosines[: len(in_table)],
                sines[: len(in_table)],
            )
            table = jnp.concatenate(blocks, axis=0)
            high = table.astype(jnp.bfloat16)
            table_ref[g, :LANES] = high
            table_ref[g, LANES:] = (table - high.astype(jnp.float32)).astype(jnp.bfloat16)
            pixel = first_pixel + iota((8, width), 0) // band * LANES
            cosine, sine = circle(pixel * modes, ring)
            blocks = unrolled(
                jnp.where(kind == 0, cosine, jnp.where(kind == 3, -cosine, -sine)),
                jnp.where(kind == 0, sine, jnp.where(kind == 3, -sine, cosine)),
                cosines[len(in_table) :],
                sines[len(in_table) :],
            )
            turn_ref[g] = jnp.concatenate(blocks, axis=0)

    return body


def fourier_kernel(maps, band, pieces, owned, copies, chunk, chunks, step):
    rows = 2 * pieces * band
    tiles = pieces * band // 8
    lines = 2 * maps
    group = 8 // owned

    def body(sky_ref, mask_ref, table_ref, turn_ref, out_ref, line_ref):
        lower = iota((8, LANES), 0) < owned

        def run(g):
            for first in range(0, maps, step):
                values = [
                    sky_ref[x * rows : (x + 1) * rows] * mask_ref[...]
                    for x in range(first, first + step)
                ]
                values = jnp.concatenate(values, axis=0)
                wide = jnp.concatenate([values, values], axis=1)
                product = jnp.dot(wide, table_ref[g], preferred_element_type=jnp.float32)
                for x in range(step):
                    totals = []
                    for h in range(2):
                        total = None
                        for t in range(tiles):
                            at = ((x * 2 + h) * tiles + t) * 8
                            term = product[at : at + 8] * turn_ref[g, t * 8 : t * 8 + 8]
                            total = term if total is None else total + term
                        totals.append(total)
                    north, south = totals
                    line_ref[pl.ds(first + x, 8, stride=lines)] = north + south
                    line_ref[pl.ds(maps + first + x, 8, stride=lines)] = north - south
            gathered = line_ref[: band * lines]
            for piece in range(1, 8 // band):
                gathered = gathered + line_ref[piece * band * lines : (piece + 1) * band * lines]
            turned = gathered.T
            real = turned[:chunk] + turned[chunk : 2 * chunk]
            imag = turned[2 * chunk : 3 * chunk] + turned[3 * chunk :]
            both = jnp.concatenate([real, imag], axis=1)
            tile = copies // group
            for i in range(chunk // 8):
                value = both[i * 8 : i * 8 + 8]
                other = pltpu.roll(value, owned, 0)
                ready = (jnp.where(lower, value, other), jnp.where(lower, other, value))
                for o in range(group):
                    for c in range(tile):
                        at = ((g * (chunk // 8) + i) * group + o) * tile + c
                        out_ref[pl.ds(at * 8, 8)] = ready[o]

        if chunks == 1:
            run(0)
        else:
            lax.fori_loop(0, chunks, lambda g, _: run(g), None)

    return body


def legendre_kernel(maps, band, owned, blocks, copies, degrees, ring):
    cycles = blocks * band
    depth = owned * cycles
    lines = 2 * maps
    half = LANES // 2
    tile = copies * owned // 8
    columns = degrees // LANES

    def body(sums_ref, aux_ref, legendre_ref, out_ref):
        lane = iota((8, LANES), 1)
        lower = iota((8, LANES), 0) < owned
        cycle = lane // lines % band
        is_first = cycle == 0
        is_last = cycle == band - 1
        mirror = jnp.where(lane // maps % 2 == 0, 1.0, -1.0)

        single = []
        for b in range(blocks):
            total = sums_ref[b * tile * 8 : b * tile * 8 + 8]
            for i in range(1, tile):
                total = total + sums_ref[(b * tile + i) * 8 : (b * tile + i) * 8 + 8]
            single.append(total + pltpu.roll(total, owned, 0))
        none = jnp.zeros((8, LANES), jnp.float32)

        def pair(b):
            at = lambda i: single[i] if 0 <= i < blocks else none
            return jnp.where(lower, at(b), at(b + 1))

        def moved(value, shift):
            return pltpu.roll(value, shift % LANES, 1)

        folded = []
        for b in range(0, blocks, 2):
            here = pair(b)
            prior = jnp.where(is_last, pair(b - 1), here)
            later = jnp.where(is_first, pair(b + 1), here)
            swapped = moved(here, half)
            up, up_swapped = moved(prior, lines), moved(prior, lines + half)
            down, down_swapped = moved(later, -lines), moved(later, half - lines)
            above = jnp.where(is_first, up_swapped, up)
            above_swapped = jnp.where(is_first, up, up_swapped)
            below = jnp.where(is_last, down_swapped, down)
            below_swapped = jnp.where(is_last, down, down_swapped)
            if b + 2 == blocks:
                equator = is_last & ~lower
                below = jnp.where(equator, mirror * here, below)
                below_swapped = jnp.where(equator, mirror * swapped, below_swapped)
            folded.append(
                aux_ref[0] * here
                + aux_ref[1] * (above + below)
                + aux_ref[2] * swapped
                + aux_ref[3] * (above_swapped + below_swapped)
            )
        folded = jnp.concatenate(folded, axis=0).astype(jnp.bfloat16)

        row = iota((blocks * owned, depth), 0)
        column = iota((blocks * owned, depth), 1)
        spread = (row // owned == (column // band) % blocks) & (row % owned == column // cycles)
        spread = jnp.where(spread, 1.0, 0.0).astype(jnp.bfloat16)
        across = lax.dot_general(
            folded, spread, (((0,), (0,)), ((), ())), preferred_element_type=jnp.float32
        )
        column = iota((lines, depth), 1)
        parts = []
        for part in range(2):
            chosen = across[part * half : part * half + lines]
            for k in range(1, band):
                at = part * half + k * lines
                chosen = jnp.where(column % band == k, across[at : at + lines], chosen)
            parts.append(chosen)
        weights = []
        for s in range(owned):
            for part in range(2):
                weights.append(jnp.where(column // cycles == s, parts[part], 0.0))
        weights = jnp.concatenate(weights, axis=0).astype(jnp.bfloat16)
        sums = jnp.dot(weights, legendre_ref[...], preferred_element_type=jnp.float32)

        first = lax.axis_index("lblk") * degrees
        for s in range(owned):
            mode = jnp.broadcast_to(aux_ref[4, s : s + 1], (maps, LANES)).astype(jnp.int32)
            degree = first + iota((maps, LANES), 1)
            even = ((degree + mode) & 1) == 0
            beyond = degree - mode
            for j in range(columns):
                inside = beyond >= -j * LANES
                for part in range(2):
                    at = (s * 2 + part) * lines
                    plus = sums[at : at + maps, j * LANES : (j + 1) * LANES]
                    minus = sums[at + maps : at + lines, j * LANES : (j + 1) * LANES]
                    value = jnp.where(inside, jnp.where(even, plus, minus), 0.0)
                    at = (part * columns + j) * owned + s
                    out_ref[pl.ds(at, maps, stride=2 * columns * owned)] = value

    return body


def on_chip(value):
    return pltpu.with_memory_space_constraint(value, pltpu.VMEM)


def local(sky, arc_start, arc_count, owner_modes, legendre):
    maps, _, band, quarter = sky.shape
    slots = owner_modes.shape[0]
    owned, groups, _, degrees = legendre.shape
    blocks, copies = lax.axis_size("blk"), lax.axis_size("lblk")
    ring = quarter * copies
    chunk = min(slots, LANES // 4)
    chunks = slots // chunk
    room = pltpu.CompilerParams(vmem_limit_bytes=28 * 2**20 if chunks > 1 else None)
    pieces = quarter // LANES
    sky_rows = sky.reshape(maps, 2, band, pieces, LANES).transpose(0, 1, 3, 2, 4)
    sky_rows = sky_rows.reshape(maps * 2 * pieces * band, LANES)
    scalars = pl.BlockSpec(memory_space=pltpu.SMEM)
    whole = pl.BlockSpec(memory_space=pltpu.VMEM)
    mask, table, turn, aux = pl.pallas_call(
        table_kernel(band, quarter, ring, owned, chunk),
        out_shape=(
            pltpu.VMEM((2 * pieces * band, LANES), jnp.bfloat16),
            pltpu.VMEM((chunks, 2 * LANES, 4 * chunk), jnp.bfloat16),
            pltpu.VMEM((chunks, pieces * band, 4 * chunk), jnp.float32),
            pltpu.VMEM((5, 8, LANES), jnp.float32),
        ),
        in_specs=[scalars] * 3 + [whole],
        out_specs=(whole,) * 4,
        cost_estimate=pl.CostEstimate(flops=10**9, bytes_accessed=4 * 10**6, transcendentals=10**6),
        compiler_params=room,
        name="tables",
    )(arc_start, arc_count, owner_modes, owner_modes.reshape(chunks, 1, chunk))
    partial = pl.pallas_call(
        fourier_kernel(maps, band, pieces, owned, copies, chunk, chunks, STEP),
        out_shape=pltpu.VMEM((blocks * copies * owned, LANES), jnp.float32),
        in_specs=[whole] * 4,
        out_specs=whole,
        scratch_shapes=[pltpu.VMEM((8 * 2 * maps, LANES), jnp.float32)],
        compiler_params=room,
        name="fourier",
    )(*(on_chip(v) for v in (sky_rows, mask, table, turn)))
    partial = partial.reshape(blocks * copies, owned, LANES)
    received = lax.all_to_all(partial, ("blk", "lblk"), split_axis=0, concat_axis=0, tiled=True)
    legendre, received = lax.optimization_barrier((legendre, received))
    legendre_rows = legendre.reshape(owned * groups * band, degrees)
    received = received.reshape(blocks * copies * owned, LANES)
    columns = degrees // LANES
    result = pl.pallas_call(
        legendre_kernel(maps, band, owned, blocks, copies, degrees, ring),
        out_shape=jax.ShapeDtypeStruct((maps * 2 * columns * owned, LANES), jnp.float32),
        in_specs=[whole] * 3,
        out_specs=whole,
        compiler_params=room,
        name="legendre",
    )(on_chip(received), on_chip(aux), on_chip(legendre_rows))
    result = result.reshape(maps, 2, columns, owned, LANES).transpose(0, 1, 3, 2, 4)
    return result.reshape(maps, 2, owned, degrees)


def solution(mesh):
    return jax.shard_map(
        local,
        mesh=mesh,
        in_specs=(
            P(None, None, "blk", "lblk"),
            P(None, "blk"),
            P(None, "blk"),
            P(),
            P("blk", None, None, "lblk"),
        ),
        out_specs=P(None, None, "blk", "lblk"),
        check_vma=False,
    )
```

```python
import math

import jax
import jax.numpy as jnp
from jax import lax
from jax.experimental import pallas as pl
from jax.experimental.pallas import tpu as pltpu
from jax.sharding import PartitionSpec as P

DIFFUSION = 0.2
LANES = 128
STEP = 4

COS_TERMS = (1.0, -1.0 / 2, 1.0 / 24, -1.0 / 720, 1.0 / 40320, -1.0 / 3628800)
SIN_TERMS = (1.0, -1.0 / 6, 1.0 / 120, -1.0 / 5040, 1.0 / 362880)


def horner(terms, square):
    total = jnp.full_like(square, terms[-1])
    for term in terms[-2::-1]:
        total = total * square + term
    return total


def circle(index, turn):
    index = index & (turn - 1)
    quadrant = (index * 4 + turn // 2) >> (turn.bit_length() - 1)
    rest = (index - quadrant * (turn // 4)).astype(jnp.float32) * (2.0 * math.pi / turn)
    square = rest * rest
    cosine = horner(COS_TERMS, square)
    sine = rest * horner(SIN_TERMS, square)
    odd = (quadrant & 1) == 1
    swapped_cos = jnp.where(odd, sine, cosine)
    swapped_sin = jnp.where(odd, cosine, sine)
    cos_sign = ((quadrant + 1) & 2) == 2
    sin_sign = (quadrant & 2) == 2
    return (
        jnp.where(cos_sign, -swapped_cos, swapped_cos),
        jnp.where(sin_sign, -swapped_sin, swapped_sin),
    )


def iota(shape, axis):
    return lax.broadcasted_iota(jnp.int32, shape, axis)


def powers(first, count):
    return [first << i for i in range(count.bit_length() - 1)]


def rotations(index, lane_modes, ring):
    amount = jnp.zeros((len(index), 1), jnp.int32)
    for i, value in enumerate(index):
        amount = jnp.where(iota(amount.shape, 0) == i, value, amount)
    return circle(amount * lane_modes, ring)


def unrolled(first, second, cosines, sines):
    blocks = [(first, second)]
    for i in range(cosines.shape[0]):
        cosine, sine = cosines[i : i + 1], sines[i : i + 1]
        blocks += [(f * cosine - s * sine, s * cosine + f * sine) for f, s in blocks]
    return [f for f, _ in blocks]


def table_kernel(band, quarter, ring, owned, chunk):
    pieces = quarter // LANES
    width = 4 * chunk

    def body(start_ref, count_ref, modes_ref, lane_modes_ref, mask_ref, table_ref, turn_ref, aux_ref):
        first_pixel = lax.axis_index("lblk") * quarter
        block = lax.axis_index("blk")
        row = iota((8, LANES), 0)
        lane = iota((8, LANES), 1)
        mine = jnp.zeros((8, LANES), jnp.int32)
        for s in range(owned):
            mine = jnp.where(row % owned == s, modes_ref[block * owned + s], mine)
        half = LANES // 2
        odd = (lane // (half // band)) % band % 2
        scale = DIFFUSION / math.sqrt(ring)
        step_cos, _ = circle(mine, ring)
        turn_cos, turn_sin = circle(mine * odd, 2 * ring)
        turn_sin = jnp.where(lane < half, turn_sin, -turn_sin)
        centre = scale * (1.0 + 2.0 * step_cos)
        aux_ref[0] = turn_cos * centre
        aux_ref[1] = turn_cos * scale
        aux_ref[2] = turn_sin * centre
        aux_ref[3] = turn_sin * scale
        aux_ref[4] = mine.astype(jnp.float32)

        masks = []
        for h in range(2):
            start = jnp.zeros((8, LANES), jnp.int32)
            count = jnp.zeros((8, LANES), jnp.int32)
            for k in range(band):
                start = jnp.where(row % band == k, start_ref[h, k], start)
                count = jnp.where(row % band == k, count_ref[h, k], count)
            shifted = first_pixel + (row // band) * LANES + lane - start
            for t in range(pieces * band // 8):
                offset = (shifted + t * (8 // band) * LANES) & (ring - 1)
                masks.append(jnp.where(offset < count, 1.0, 0.0))
        mask_ref[...] = jnp.concatenate(masks, axis=0).astype(jnp.bfloat16)

        kind = iota((1, width), 1) // chunk
        step = 8 // band * LANES
        in_table = powers(8, LANES // 8)
        in_turn = powers(step, quarter // step)
        for g in range(lane_modes_ref.shape[0]):
            modes = jnp.concatenate([lane_modes_ref[g]] * 4, axis=1)
            cosines, sines = rotations(in_table + in_turn, modes, ring)
            cosine, sine = circle(iota((8, width), 0) * modes, ring)
            is_cos = kind % 2 == 0
            blocks = unrolled(
                jnp.where(is_cos, cosine, sine),
                jnp.where(is_cos, sine, -cosine),
                cosines[: len(in_table)],
                sines[: len(in_table)],
            )
            table_ref[g] = jnp.concatenate(blocks, axis=0).astype(jnp.bfloat16)
            pixel = first_pixel + iota((8, width), 0) // band * LANES
            cosine, sine = circle(pixel * modes, ring)
            blocks = unrolled(
                jnp.where(kind == 0, cosine, jnp.where(kind == 3, -cosine, -sine)),
                jnp.where(kind == 0, sine, jnp.where(kind == 3, -sine, cosine)),
                cosines[len(in_table) :],
                sines[len(in_table) :],
            )
            turn_ref[g] = jnp.concatenate(blocks, axis=0)

    return body


def fourier_kernel(maps, band, pieces, owned, copies, chunk, chunks, step):
    rows = 2 * pieces * band
    tiles = pieces * band // 8
    lines = 2 * maps
    group = 8 // owned

    def body(sky_ref, mask_ref, table_ref, turn_ref, out_ref, line_ref):
        lower = iota((8, LANES), 0) < owned

        def run(g):
            for first in range(0, maps, step):
                masked = [
                    sky_ref[x * rows : (x + 1) * rows] * mask_ref[...]
                    for x in range(first, first + step)
                ]
                product = jnp.dot(
                    jnp.concatenate(masked, axis=0), table_ref[g], preferred_element_type=jnp.float32
                )
                for x in range(step):
                    totals = []
                    for h in range(2):
                        terms = []
                        for t in range(tiles):
                            at = ((x * 2 + h) * tiles + t) * 8
                            terms.append(product[at : at + 8] * turn_ref[g, t * 8 : t * 8 + 8])
                        while len(terms) > 1:
                            terms = [a + b for a, b in zip(terms[::2], terms[1::2], strict=True)]
                        totals += terms
                    north, south = totals
                    line_ref[pl.ds(first + x, 8, stride=lines)] = north + south
                    line_ref[pl.ds(maps + first + x, 8, stride=lines)] = north - south
            gathered = line_ref[: band * lines]
            for piece in range(1, 8 // band):
                gathered = gathered + line_ref[piece * band * lines : (piece + 1) * band * lines]
            turned = gathered.T
            real = turned[:chunk] + turned[chunk : 2 * chunk]
            imag = turned[2 * chunk : 3 * chunk] + turned[3 * chunk :]
            both = jnp.concatenate([real, imag], axis=1)
            tile = copies // group
            for i in range(chunk // 8):
                value = both[i * 8 : i * 8 + 8]
                other = pltpu.roll(value, owned, 0)
                ready = (jnp.where(lower, value, other), jnp.where(lower, other, value))
                for o in range(group):
                    for c in range(tile):
                        at = ((g * (chunk // 8) + i) * group + o) * tile + c
                        out_ref[pl.ds(at * 8, 8)] = ready[o]

        if chunks == 1:
            run(0)
        else:
            lax.fori_loop(0, chunks, lambda g, _: run(g), None)

    return body


def legendre_kernel(maps, band, owned, blocks, copies, degrees, ring):
    cycles = blocks * band
    depth = owned * cycles
    lines = 2 * maps
    half = LANES // 2
    tile = copies * owned // 8
    columns = degrees // LANES

    def body(sums_ref, aux_ref, legendre_ref, out_ref, line_ref):
        lane = iota((8, LANES), 1)
        lower = iota((8, LANES), 0) < owned
        cycle = lane // lines % band
        is_first = cycle == 0
        is_last = cycle == band - 1
        mirror = jnp.where(lane // maps % 2 == 0, 1.0, -1.0)

        single = []
        for b in range(blocks):
            total = sums_ref[b * tile * 8 : b * tile * 8 + 8]
            for i in range(1, tile):
                total = total + sums_ref[(b * tile + i) * 8 : (b * tile + i) * 8 + 8]
            single.append(total + pltpu.roll(total, owned, 0))
        none = jnp.zeros((8, LANES), jnp.float32)

        def pair(b):
            at = lambda i: single[i] if 0 <= i < blocks else none
            return jnp.where(lower, at(b), at(b + 1))

        def moved(value, shift):
            return pltpu.roll(value, shift % LANES, 1)

        folded = []
        for b in range(0, blocks, 2):
            here = pair(b)
            prior = jnp.where(is_last, pair(b - 1), here)
            later = jnp.where(is_first, pair(b + 1), here)
            swapped = moved(here, half)
            up, up_swapped = moved(prior, lines), moved(prior, lines + half)
            down, down_swapped = moved(later, -lines), moved(later, half - lines)
            above = jnp.where(is_first, up_swapped, up)
            above_swapped = jnp.where(is_first, up, up_swapped)
            below = jnp.where(is_last, down_swapped, down)
            below_swapped = jnp.where(is_last, down, down_swapped)
            if b + 2 == blocks:
                equator = is_last & ~lower
                below = jnp.where(equator, mirror * here, below)
                below_swapped = jnp.where(equator, mirror * swapped, below_swapped)
            folded.append(
                aux_ref[0] * here
                + aux_ref[1] * (above + below)
                + aux_ref[2] * swapped
                + aux_ref[3] * (above_swapped + below_swapped)
            )
        folded = jnp.concatenate(folded, axis=0).astype(jnp.bfloat16)

        row = iota((blocks * owned, depth), 0)
        column = iota((blocks * owned, depth), 1)
        spread = (row // owned == (column // band) % blocks) & (row % owned == column // cycles)
        spread = jnp.where(spread, 1.0, 0.0).astype(jnp.bfloat16)
        across = lax.dot_general(
            folded, spread, (((0,), (0,)), ((), ())), preferred_element_type=jnp.float32
        )
        column = iota((lines, depth), 1)
        parts = []
        for part in range(2):
            chosen = across[part * half : part * half + lines]
            for k in range(1, band):
                at = part * half + k * lines
                chosen = jnp.where(column % band == k, across[at : at + lines], chosen)
            parts.append(chosen)
        for part in range(2):
            line_ref[part * lines : (part + 1) * lines] = parts[part]
        mine = iota((8, depth), 1) // cycles == iota((8, depth), 0) % owned
        weights = []
        for i in range(lines):
            value = jnp.where(
                iota((8, depth), 0) < owned,
                line_ref[pl.ds(i, 8, stride=0)],
                line_ref[pl.ds(lines + i, 8, stride=0)],
            )
            weights.append(jnp.where(mine, value, 0.0))
        weights = jnp.concatenate(weights, axis=0).astype(jnp.bfloat16)
        sums = jnp.dot(weights, legendre_ref[...], preferred_element_type=jnp.float32)

        mode = aux_ref[4].astype(jnp.int32)
        degree = lax.axis_index("lblk") * degrees + lane
        even = ((degree + mode) & 1) == 0
        beyond = degree - mode
        for j in range(0, columns, 2):
            inside = [beyond >= -(j + i) * LANES for i in range(2)]
            for x in range(maps):
                near, far = (
                    jnp.where(
                        inside[i],
                        jnp.where(
                            even,
                            sums[x * 8 : x * 8 + 8, (j + i) * LANES : (j + i + 1) * LANES],
                            sums[(maps + x) * 8 : (maps + x) * 8 + 8, (j + i) * LANES : (j + i + 1) * LANES],
                        ),
                        0.0,
                    )
                    for i in range(2)
                )
                at = (x * 2 * columns + j) * owned
                out_ref[pl.ds(at, 8)] = jnp.where(lower, near, pltpu.roll(far, owned, 0))
                at += columns * owned
                out_ref[pl.ds(at, 8)] = jnp.where(lower, pltpu.roll(near, owned, 0), far)

    return body


def on_chip(value):
    return pltpu.with_memory_space_constraint(value, pltpu.VMEM)


def local(sky, arc_start, arc_count, owner_modes, legendre):
    maps, _, band, quarter = sky.shape
    slots = owner_modes.shape[0]
    owned, groups, _, degrees = legendre.shape
    blocks, copies = lax.axis_size("blk"), lax.axis_size("lblk")
    ring = quarter * copies
    chunk = min(slots, LANES // 4)
    chunks = slots // chunk
    room = pltpu.CompilerParams(vmem_limit_bytes=28 * 2**20 if chunks > 1 else None)
    pieces = quarter // LANES
    sky_rows = sky.reshape(maps, 2, band, pieces, LANES).transpose(0, 1, 3, 2, 4)
    sky_rows = sky_rows.reshape(maps * 2 * pieces * band, LANES)
    scalars = pl.BlockSpec(memory_space=pltpu.SMEM)
    whole = pl.BlockSpec(memory_space=pltpu.VMEM)
    mask, table, turn, aux = pl.pallas_call(
        table_kernel(band, quarter, ring, owned, chunk),
        out_shape=(
            pltpu.VMEM((2 * pieces * band, LANES), jnp.bfloat16),
            pltpu.VMEM((chunks, LANES, 4 * chunk), jnp.bfloat16),
            pltpu.VMEM((chunks, pieces * band, 4 * chunk), jnp.float32),
            pltpu.VMEM((5, 8, LANES), jnp.float32),
        ),
        in_specs=[scalars] * 3 + [whole],
        out_specs=(whole,) * 4,
        cost_estimate=pl.CostEstimate(flops=10**9, bytes_accessed=4 * 10**6, transcendentals=10**6),
        compiler_params=room,
        name="tables",
    )(arc_start, arc_count, owner_modes, owner_modes.reshape(chunks, 1, chunk))
    partial = pl.pallas_call(
        fourier_kernel(maps, band, pieces, owned, copies, chunk, chunks, STEP),
        out_shape=pltpu.VMEM((blocks * copies * owned, LANES), jnp.float32),
        in_specs=[whole] * 4,
        out_specs=whole,
        scratch_shapes=[pltpu.VMEM((8 * 2 * maps, LANES), jnp.float32)],
        compiler_params=room,
        name="fourier",
    )(*(on_chip(v) for v in (sky_rows, mask, table, turn)))
    partial = partial.reshape(blocks * copies, owned, LANES)
    received = lax.all_to_all(partial, ("blk", "lblk"), split_axis=0, concat_axis=0, tiled=True)
    legendre, received = lax.optimization_barrier((legendre, received))
    legendre_rows = legendre.reshape(owned * groups * band, degrees)
    received = received.reshape(blocks * copies * owned, LANES)
    columns = degrees // LANES
    result = pl.pallas_call(
        legendre_kernel(maps, band, owned, blocks, copies, degrees, ring),
        out_shape=jax.ShapeDtypeStruct((maps * 2 * columns * owned, LANES), jnp.float32),
        in_specs=[whole] * 3,
        out_specs=whole,
        scratch_shapes=[pltpu.VMEM((4 * maps, owned * groups * band), jnp.float32)],
        compiler_params=room,
        name="legendre",
    )(on_chip(received), on_chip(aux), on_chip(legendre_rows))
    result = result.reshape(maps, 2, columns, owned, LANES).transpose(0, 1, 3, 2, 4)
    return result.reshape(maps, 2, owned, degrees)


def solution(mesh):
    return jax.shard_map(
        local,
        mesh=mesh,
        in_specs=(
            P(None, None, "blk", "lblk"),
            P(None, "blk"),
            P(None, "blk"),
            P(),
            P("blk", None, None, "lblk"),
        ),
        out_specs=P(None, None, "blk", "lblk"),
        check_vma=False,
    )
```

```python
import math

import jax
import jax.numpy as jnp
from jax import lax
from jax.experimental import pallas as pl
from jax.experimental.pallas import tpu as pltpu
from jax.sharding import PartitionSpec as P

DIFFUSION = 0.2
LANES = 128
STEP = 4

COS_TERMS = (1.0, -1.0 / 2, 1.0 / 24, -1.0 / 720, 1.0 / 40320, -1.0 / 3628800)
SIN_TERMS = (1.0, -1.0 / 6, 1.0 / 120, -1.0 / 5040, 1.0 / 362880)


def horner(terms, square):
    total = jnp.full_like(square, terms[-1])
    for term in terms[-2::-1]:
        total = total * square + term
    return total


def circle(index, turn):
    index = index & (turn - 1)
    quadrant = (index * 4 + turn // 2) >> (turn.bit_length() - 1)
    rest = (index - quadrant * (turn // 4)).astype(jnp.float32) * (2.0 * math.pi / turn)
    square = rest * rest
    cosine = horner(COS_TERMS, square)
    sine = rest * horner(SIN_TERMS, square)
    odd = (quadrant & 1) == 1
    swapped_cos = jnp.where(odd, sine, cosine)
    swapped_sin = jnp.where(odd, cosine, sine)
    cos_sign = ((quadrant + 1) & 2) == 2
    sin_sign = (quadrant & 2) == 2
    return (
        jnp.where(cos_sign, -swapped_cos, swapped_cos),
        jnp.where(sin_sign, -swapped_sin, swapped_sin),
    )


def iota(shape, axis):
    return lax.broadcasted_iota(jnp.int32, shape, axis)


def powers(first, count):
    return [first << i for i in range(count.bit_length() - 1)]


def rotations(index, lane_modes, ring):
    amount = jnp.zeros((len(index), 1), jnp.int32)
    for i, value in enumerate(index):
        amount = jnp.where(iota(amount.shape, 0) == i, value, amount)
    return circle(amount * lane_modes, ring)


def unrolled(first, second, cosines, sines):
    blocks = [(first, second)]
    for i in range(cosines.shape[0]):
        cosine, sine = cosines[i : i + 1], sines[i : i + 1]
        blocks += [(f * cosine - s * sine, s * cosine + f * sine) for f, s in blocks]
    return [f for f, _ in blocks]


def table_kernel(band, quarter, ring, owned, chunk):
    pieces = quarter // LANES
    width = 4 * chunk

    def body(start_ref, count_ref, modes_ref, lane_modes_ref, mask_ref, table_ref, turn_ref, aux_ref):
        first_pixel = lax.axis_index("lblk") * quarter
        block = lax.axis_index("blk")
        row = iota((8, LANES), 0)
        lane = iota((8, LANES), 1)
        mine = jnp.zeros((8, LANES), jnp.int32)
        for s in range(owned):
            mine = jnp.where(row % owned == s, modes_ref[block * owned + s], mine)
        half = LANES // 2
        odd = (lane // (half // band)) % band % 2
        scale = DIFFUSION / math.sqrt(ring)
        step_cos, _ = circle(mine, ring)
        turn_cos, turn_sin = circle(mine * odd, 2 * ring)
        turn_sin = jnp.where(lane < half, turn_sin, -turn_sin)
        centre = scale * (1.0 + 2.0 * step_cos)
        aux_ref[0] = turn_cos * centre
        aux_ref[1] = turn_cos * scale
        aux_ref[2] = turn_sin * centre
        aux_ref[3] = turn_sin * scale
        aux_ref[4] = mine.astype(jnp.float32)

        masks = []
        for h in range(2):
            start = jnp.zeros((8, LANES), jnp.int32)
            count = jnp.zeros((8, LANES), jnp.int32)
            for k in range(band):
                start = jnp.where(row % band == k, start_ref[h, k], start)
                count = jnp.where(row % band == k, count_ref[h, k], count)
            shifted = first_pixel + (row // band) * LANES + lane - start
            for t in range(pieces * band // 8):
                offset = (shifted + t * (8 // band) * LANES) & (ring - 1)
                masks.append(jnp.where(offset < count, 1.0, 0.0))
        mask_ref[...] = jnp.concatenate(masks, axis=0).astype(jnp.bfloat16)

        kind = iota((1, width), 1) // chunk
        step = 8 // band * LANES
        in_table = powers(8, LANES // 8)
        in_turn = powers(step, quarter // step)
        for g in range(lane_modes_ref.shape[0]):
            modes = jnp.concatenate([lane_modes_ref[g]] * 4, axis=1)
            cosines, sines = rotations(in_table + in_turn, modes, ring)
            cosine, sine = circle(iota((8, width), 0) * modes, ring)
            is_cos = kind % 2 == 0
            blocks = unrolled(
                jnp.where(is_cos, cosine, sine),
                jnp.where(is_cos, sine, -cosine),
                cosines[: len(in_table)],
                sines[: len(in_table)],
            )
            table_ref[g] = jnp.concatenate(blocks, axis=0).astype(jnp.bfloat16)
            pixel = first_pixel + iota((8, width), 0) // band * LANES
            cosine, sine = circle(pixel * modes, ring)
            blocks = unrolled(
                jnp.where(kind == 0, cosine, jnp.where(kind == 3, -cosine, -sine)),
                jnp.where(kind == 0, sine, jnp.where(kind == 3, -sine, cosine)),
                cosines[len(in_table) :],
                sines[len(in_table) :],
            )
            turn_ref[g] = jnp.concatenate(blocks, axis=0)

    return body


def fourier_kernel(maps, band, pieces, owned, copies, chunk, chunks, step):
    rows = 2 * pieces * band
    tiles = pieces * band // 8
    lines = 2 * maps
    group = 8 // owned

    def body(sky_ref, mask_ref, table_ref, turn_ref, out_ref, line_ref):
        lower = iota((8, LANES), 0) < owned

        def run(g):
            for first in range(0, maps, step):
                masked = [
                    sky_ref[x * rows : (x + 1) * rows] * mask_ref[...]
                    for x in range(first, first + step)
                ]
                product = jnp.dot(
                    jnp.concatenate(masked, axis=0), table_ref[g], preferred_element_type=jnp.float32
                )
                for x in range(step):
                    totals = []
                    for h in range(2):
                        terms = []
                        for t in range(tiles):
                            at = ((x * 2 + h) * tiles + t) * 8
                            terms.append(product[at : at + 8] * turn_ref[g, t * 8 : t * 8 + 8])
                        while len(terms) > 1:
                            terms = [a + b for a, b in zip(terms[::2], terms[1::2], strict=True)]
                        totals += terms
                    north, south = totals
                    line_ref[pl.ds(first + x, 8, stride=lines)] = north + south
                    line_ref[pl.ds(maps + first + x, 8, stride=lines)] = north - south
            gathered = line_ref[: band * lines]
            for piece in range(1, 8 // band):
                gathered = gathered + line_ref[piece * band * lines : (piece + 1) * band * lines]
            turned = gathered.T
            real = turned[:chunk] + turned[chunk : 2 * chunk]
            imag = turned[2 * chunk : 3 * chunk] + turned[3 * chunk :]
            both = jnp.concatenate([real, imag], axis=1)
            tile = copies // group
            for i in range(chunk // 8):
                value = both[i * 8 : i * 8 + 8]
                other = pltpu.roll(value, owned, 0)
                ready = (jnp.where(lower, value, other), jnp.where(lower, other, value))
                for o in range(group):
                    for c in range(tile):
                        at = ((g * (chunk // 8) + i) * group + o) * tile + c
                        out_ref[pl.ds(at * 8, 8)] = ready[o]

        if chunks == 1:
            run(0)
        else:
            lax.fori_loop(0, chunks, lambda g, _: run(g), None)

    return body


def legendre_kernel(maps, band, owned, blocks, copies, degrees, ring):
    cycles = blocks * band
    depth = owned * cycles
    lines = 2 * maps
    half = LANES // 2
    tile = copies * owned // 8
    columns = degrees // LANES

    def body(sums_ref, aux_ref, legendre_ref, out_ref, line_ref):
        lane = iota((8, LANES), 1)
        lower = iota((8, LANES), 0) < owned
        cycle = lane // lines % band
        is_first = cycle == 0
        is_last = cycle == band - 1
        mirror = jnp.where(lane // maps % 2 == 0, 1.0, -1.0)

        single = []
        for b in range(blocks):
            total = sums_ref[b * tile * 8 : b * tile * 8 + 8]
            for i in range(1, tile):
                total = total + sums_ref[(b * tile + i) * 8 : (b * tile + i) * 8 + 8]
            single.append(total + pltpu.roll(total, owned, 0))
        none = jnp.zeros((8, LANES), jnp.float32)

        def pair(b):
            at = lambda i: single[i] if 0 <= i < blocks else none
            return jnp.where(lower, at(b), at(b + 1))

        def moved(value, shift):
            return pltpu.roll(value, shift % LANES, 1)

        folded = []
        for b in range(0, blocks, 2):
            here = pair(b)
            prior = jnp.where(is_last, pair(b - 1), here)
            later = jnp.where(is_first, pair(b + 1), here)
            swapped = moved(here, half)
            up, up_swapped = moved(prior, lines), moved(prior, lines + half)
            down, down_swapped = moved(later, -lines), moved(later, half - lines)
            above = jnp.where(is_first, up_swapped, up)
            above_swapped = jnp.where(is_first, up, up_swapped)
            below = jnp.where(is_last, down_swapped, down)
            below_swapped = jnp.where(is_last, down, down_swapped)
            if b + 2 == blocks:
                equator = is_last & ~lower
                below = jnp.where(equator, mirror * here, below)
                below_swapped = jnp.where(equator, mirror * swapped, below_swapped)
            folded.append(
                aux_ref[0] * here
                + aux_ref[1] * (above + below)
                + aux_ref[2] * swapped
                + aux_ref[3] * (above_swapped + below_swapped)
            )
        folded = jnp.concatenate(folded, axis=0).astype(jnp.bfloat16)

        row = iota((blocks * owned, depth), 0)
        column = iota((blocks * owned, depth), 1)
        spread = (row // owned == (column // band) % blocks) & (row % owned == column // cycles)
        spread = jnp.where(spread, 1.0, 0.0).astype(jnp.bfloat16)
        across = lax.dot_general(
            folded, spread, (((0,), (0,)), ((), ())), preferred_element_type=jnp.float32
        )
        column = iota((lines, depth), 1)
        parts = []
        for part in range(2):
            chosen = across[part * half : part * half + lines]
            for k in range(1, band):
                at = part * half + k * lines
                chosen = jnp.where(column % band == k, across[at : at + lines], chosen)
            parts.append(chosen)
        for part in range(2):
            line_ref[part * lines : (part + 1) * lines] = parts[part]
        mine = iota((8, depth), 1) // cycles == iota((8, depth), 0) % owned
        weights = []
        for i in range(lines):
            value = jnp.where(
                iota((8, depth), 0) < owned,
                jnp.broadcast_to(line_ref[i : i + 1], (8, depth)),
                jnp.broadcast_to(line_ref[lines + i : lines + i + 1], (8, depth)),
            )
            weights.append(jnp.where(mine, value, 0.0))
        weights = jnp.concatenate(weights, axis=0).astype(jnp.bfloat16)
        sums = jnp.dot(weights, legendre_ref[...], preferred_element_type=jnp.float32)

        mode = aux_ref[4].astype(jnp.int32)
        degree = lax.axis_index("lblk") * degrees + lane
        even = ((degree + mode) & 1) == 0
        beyond = degree - mode
        for j in range(0, columns, 2):
            inside = [beyond >= -(j + i) * LANES for i in range(2)]
            for x in range(maps):
                near, far = (
                    jnp.where(
                        inside[i],
                        jnp.where(
                            even,
                            sums[x * 8 : x * 8 + 8, (j + i) * LANES : (j + i + 1) * LANES],
                            sums[(maps + x) * 8 : (maps + x) * 8 + 8, (j + i) * LANES : (j + i + 1) * LANES],
                        ),
                        0.0,
                    )
                    for i in range(2)
                )
                at = (x * 2 * columns + j) * owned
                out_ref[pl.ds(at, 8)] = jnp.where(lower, near, pltpu.roll(far, owned, 0))
                at += columns * owned
                out_ref[pl.ds(at, 8)] = jnp.where(lower, pltpu.roll(near, owned, 0), far)

    return body


def on_chip(value):
    return pltpu.with_memory_space_constraint(value, pltpu.VMEM)


def local(sky, arc_start, arc_count, owner_modes, legendre):
    maps, _, band, quarter = sky.shape
    slots = owner_modes.shape[0]
    owned, groups, _, degrees = legendre.shape
    blocks, copies = lax.axis_size("blk"), lax.axis_size("lblk")
    ring = quarter * copies
    chunk = min(slots, LANES // 4)
    chunks = slots // chunk
    room = pltpu.CompilerParams(vmem_limit_bytes=28 * 2**20 if chunks > 1 else None)
    pieces = quarter // LANES
    sky_rows = sky.reshape(maps, 2, band, pieces, LANES).transpose(0, 1, 3, 2, 4)
    sky_rows = sky_rows.reshape(maps * 2 * pieces * band, LANES)
    scalars = pl.BlockSpec(memory_space=pltpu.SMEM)
    whole = pl.BlockSpec(memory_space=pltpu.VMEM)
    mask, table, turn, aux = pl.pallas_call(
        table_kernel(band, quarter, ring, owned, chunk),
        out_shape=(
            pltpu.VMEM((2 * pieces * band, LANES), jnp.bfloat16),
            pltpu.VMEM((chunks, LANES, 4 * chunk), jnp.bfloat16),
            pltpu.VMEM((chunks, pieces * band, 4 * chunk), jnp.float32),
            pltpu.VMEM((5, 8, LANES), jnp.float32),
        ),
        in_specs=[scalars] * 3 + [whole],
        out_specs=(whole,) * 4,
        cost_estimate=pl.CostEstimate(flops=10**9, bytes_accessed=4 * 10**6, transcendentals=10**6),
        compiler_params=room,
        name="tables",
    )(arc_start, arc_count, owner_modes, owner_modes.reshape(chunks, 1, chunk))
    partial = pl.pallas_call(
        fourier_kernel(maps, band, pieces, owned, copies, chunk, chunks, STEP),
        out_shape=pltpu.VMEM((blocks * copies * owned, LANES), jnp.float32),
        in_specs=[whole] * 4,
        out_specs=whole,
        scratch_shapes=[pltpu.VMEM((8 * 2 * maps, LANES), jnp.float32)],
        compiler_params=room,
        name="fourier",
    )(*(on_chip(v) for v in (sky_rows, mask, table, turn)))
    partial = partial.reshape(blocks * copies, owned, LANES)
    received = lax.all_to_all(partial, ("blk", "lblk"), split_axis=0, concat_axis=0, tiled=True)
    legendre, received = lax.optimization_barrier((legendre, received))
    legendre_rows = legendre.reshape(owned * groups * band, degrees)
    received = received.reshape(blocks * copies * owned, LANES)
    columns = degrees // LANES
    result = pl.pallas_call(
        legendre_kernel(maps, band, owned, blocks, copies, degrees, ring),
        out_shape=jax.ShapeDtypeStruct((maps * 2 * columns * owned, LANES), jnp.float32),
        in_specs=[whole] * 3,
        out_specs=whole,
        scratch_shapes=[pltpu.VMEM((4 * maps, owned * groups * band), jnp.float32)],
        compiler_params=room,
        name="legendre",
    )(on_chip(received), on_chip(aux), on_chip(legendre_rows))
    result = result.reshape(maps, 2, columns, owned, LANES).transpose(0, 1, 3, 2, 4)
    return result.reshape(maps, 2, owned, degrees)


def solution(mesh):
    return jax.shard_map(
        local,
        mesh=mesh,
        in_specs=(
            P(None, None, "blk", "lblk"),
            P(None, "blk"),
            P(None, "blk"),
            P(),
            P("blk", None, None, "lblk"),
        ),
        out_specs=P(None, None, "blk", "lblk"),
        check_vma=False,
    )
```

```python
import math

import jax
import jax.numpy as jnp
from jax import lax
from jax.experimental import pallas as pl
from jax.experimental.pallas import tpu as pltpu
from jax.sharding import PartitionSpec as P

DIFFUSION = 0.2
LANES = 128
STEP = 4

COS_TERMS = (1.0, -1.0 / 2, 1.0 / 24, -1.0 / 720, 1.0 / 40320, -1.0 / 3628800)
SIN_TERMS = (1.0, -1.0 / 6, 1.0 / 120, -1.0 / 5040, 1.0 / 362880)


def horner(terms, square):
    total = jnp.full_like(square, terms[-1])
    for term in terms[-2::-1]:
        total = total * square + term
    return total


def circle(index, turn):
    index = index & (turn - 1)
    quadrant = (index * 4 + turn // 2) >> (turn.bit_length() - 1)
    rest = (index - quadrant * (turn // 4)).astype(jnp.float32) * (2.0 * math.pi / turn)
    square = rest * rest
    cosine = horner(COS_TERMS, square)
    sine = rest * horner(SIN_TERMS, square)
    odd = (quadrant & 1) == 1
    swapped_cos = jnp.where(odd, sine, cosine)
    swapped_sin = jnp.where(odd, cosine, sine)
    cos_sign = ((quadrant + 1) & 2) == 2
    sin_sign = (quadrant & 2) == 2
    return (
        jnp.where(cos_sign, -swapped_cos, swapped_cos),
        jnp.where(sin_sign, -swapped_sin, swapped_sin),
    )


def iota(shape, axis):
    return lax.broadcasted_iota(jnp.int32, shape, axis)


def powers(first, count):
    return [first << i for i in range(count.bit_length() - 1)]


def rotations(index, lane_modes, ring):
    amount = jnp.zeros((len(index), 1), jnp.int32)
    for i, value in enumerate(index):
        amount = jnp.where(iota(amount.shape, 0) == i, value, amount)
    return circle(amount * lane_modes, ring)


def unrolled(first, second, cosines, sines):
    blocks = [(first, second)]
    for i in range(cosines.shape[0]):
        cosine, sine = cosines[i : i + 1], sines[i : i + 1]
        blocks += [(f * cosine - s * sine, s * cosine + f * sine) for f, s in blocks]
    return [f for f, _ in blocks]


def table_kernel(band, quarter, ring, owned, chunk):
    pieces = quarter // LANES
    width = 4 * chunk

    def body(start_ref, count_ref, modes_ref, lane_modes_ref, mask_ref, table_ref, turn_ref, aux_ref):
        first_pixel = lax.axis_index("lblk") * quarter
        block = lax.axis_index("blk")
        row = iota((8, LANES), 0)
        lane = iota((8, LANES), 1)
        mine = jnp.zeros((8, LANES), jnp.int32)
        for s in range(owned):
            mine = jnp.where(row % owned == s, modes_ref[block * owned + s], mine)
        half = LANES // 2
        odd = (lane // (half // band)) % band % 2
        scale = DIFFUSION / math.sqrt(ring)
        step_cos, _ = circle(mine, ring)
        turn_cos, turn_sin = circle(mine * odd, 2 * ring)
        turn_sin = jnp.where(lane < half, turn_sin, -turn_sin)
        centre = scale * (1.0 + 2.0 * step_cos)
        aux_ref[0] = turn_cos * centre
        aux_ref[1] = turn_cos * scale
        aux_ref[2] = turn_sin * centre
        aux_ref[3] = turn_sin * scale
        aux_ref[4] = mine.astype(jnp.float32)

        masks = []
        for h in range(2):
            start = jnp.zeros((8, LANES), jnp.int32)
            count = jnp.zeros((8, LANES), jnp.int32)
            for k in range(band):
                start = jnp.where(row % band == k, start_ref[h, k], start)
                count = jnp.where(row % band == k, count_ref[h, k], count)
            shifted = first_pixel + (row // band) * LANES + lane - start
            for t in range(pieces * band // 8):
                offset = (shifted + t * (8 // band) * LANES) & (ring - 1)
                masks.append(jnp.where(offset < count, 1.0, 0.0))
        mask_ref[...] = jnp.concatenate(masks, axis=0).astype(jnp.bfloat16)

        kind = iota((1, width), 1) // chunk
        step = 8 // band * LANES
        in_table = powers(8, LANES // 8)
        in_turn = powers(step, quarter // step)
        for g in range(lane_modes_ref.shape[0]):
            modes = jnp.concatenate([lane_modes_ref[g]] * 4, axis=1)
            cosines, sines = rotations(in_table + in_turn, modes, ring)
            cosine, sine = circle(iota((8, width), 0) * modes, ring)
            is_cos = kind % 2 == 0
            blocks = unrolled(
                jnp.where(is_cos, cosine, sine),
                jnp.where(is_cos, sine, -cosine),
                cosines[: len(in_table)],
                sines[: len(in_table)],
            )
            table_ref[g] = jnp.concatenate(blocks, axis=0).astype(jnp.bfloat16)
            pixel = first_pixel + iota((8, width), 0) // band * LANES
            cosine, sine = circle(pixel * modes, ring)
            blocks = unrolled(
                jnp.where(kind == 0, cosine, jnp.where(kind == 3, -cosine, -sine)),
                jnp.where(kind == 0, sine, jnp.where(kind == 3, -sine, cosine)),
                cosines[len(in_table) :],
                sines[len(in_table) :],
            )
            turn_ref[g] = jnp.concatenate(blocks, axis=0)

    return body


def fourier_kernel(maps, band, pieces, owned, copies, chunk, chunks, step):
    rows = 2 * pieces * band
    tiles = pieces * band // 8
    lines = 2 * maps
    group = 8 // owned

    def body(sky_ref, mask_ref, table_ref, turn_ref, out_ref, line_ref):
        lower = iota((8, LANES), 0) < owned

        def run(g):
            for first in range(0, maps, step):
                masked = [
                    sky_ref[x * rows : (x + 1) * rows] * mask_ref[...]
                    for x in range(first, first + step)
                ]
                product = jnp.dot(
                    jnp.concatenate(masked, axis=0), table_ref[g], preferred_element_type=jnp.float32
                )
                for x in range(step):
                    totals = []
                    for h in range(2):
                        terms = []
                        for t in range(tiles):
                            at = ((x * 2 + h) * tiles + t) * 8
                            terms.append(product[at : at + 8] * turn_ref[g, t * 8 : t * 8 + 8])
                        while len(terms) > 1:
                            terms = [a + b for a, b in zip(terms[::2], terms[1::2], strict=True)]
                        totals += terms
                    north, south = totals
                    line_ref[pl.ds(first + x, 8, stride=lines)] = north + south
                    line_ref[pl.ds(maps + first + x, 8, stride=lines)] = north - south
            gathered = line_ref[: band * lines]
            for piece in range(1, 8 // band):
                gathered = gathered + line_ref[piece * band * lines : (piece + 1) * band * lines]
            turned = gathered.T
            real = turned[:chunk] + turned[chunk : 2 * chunk]
            imag = turned[2 * chunk : 3 * chunk] + turned[3 * chunk :]
            both = jnp.concatenate([real, imag], axis=1)
            tile = copies // group
            for i in range(chunk // 8):
                value = both[i * 8 : i * 8 + 8]
                other = pltpu.roll(value, owned, 0)
                ready = (jnp.where(lower, value, other), jnp.where(lower, other, value))
                for o in range(group):
                    for c in range(tile):
                        at = ((g * (chunk // 8) + i) * group + o) * tile + c
                        out_ref[pl.ds(at * 8, 8)] = ready[o]

        if chunks == 1:
            run(0)
        else:
            lax.fori_loop(0, chunks, lambda g, _: run(g), None)

    return body


def legendre_kernel(maps, band, owned, blocks, copies, degrees, ring):
    cycles = blocks * band
    depth = owned * cycles
    lines = 2 * maps
    half = LANES // 2
    tile = copies * owned // 8
    columns = degrees // LANES

    def body(sums_ref, aux_ref, legendre_ref, out_ref, line_ref):
        lane = iota((8, LANES), 1)
        lower = iota((8, LANES), 0) < owned
        cycle = lane // lines % band
        is_first = cycle == 0
        is_last = cycle == band - 1
        mirror = jnp.where(lane // maps % 2 == 0, 1.0, -1.0)

        single = []
        for b in range(blocks):
            total = sums_ref[b * tile * 8 : b * tile * 8 + 8]
            for i in range(1, tile):
                total = total + sums_ref[(b * tile + i) * 8 : (b * tile + i) * 8 + 8]
            single.append(total + pltpu.roll(total, owned, 0))
        none = jnp.zeros((8, LANES), jnp.float32)

        def pair(b):
            at = lambda i: single[i] if 0 <= i < blocks else none
            return jnp.where(lower, at(b), at(b + 1))

        def moved(value, shift):
            return pltpu.roll(value, shift % LANES, 1)

        folded = []
        for b in range(0, blocks, 2):
            here = pair(b)
            prior = jnp.where(is_last, pair(b - 1), here)
            later = jnp.where(is_first, pair(b + 1), here)
            swapped = moved(here, half)
            up, up_swapped = moved(prior, lines), moved(prior, lines + half)
            down, down_swapped = moved(later, -lines), moved(later, half - lines)
            above = jnp.where(is_first, up_swapped, up)
            above_swapped = jnp.where(is_first, up, up_swapped)
            below = jnp.where(is_last, down_swapped, down)
            below_swapped = jnp.where(is_last, down, down_swapped)
            if b + 2 == blocks:
                equator = is_last & ~lower
                below = jnp.where(equator, mirror * here, below)
                below_swapped = jnp.where(equator, mirror * swapped, below_swapped)
            folded.append(
                aux_ref[0] * here
                + aux_ref[1] * (above + below)
                + aux_ref[2] * swapped
                + aux_ref[3] * (above_swapped + below_swapped)
            )
        folded = jnp.concatenate(folded, axis=0).astype(jnp.bfloat16)

        row = iota((blocks * owned, depth), 0)
        column = iota((blocks * owned, depth), 1)
        spread = (row // owned == (column // band) % blocks) & (row % owned == column // cycles)
        spread = jnp.where(spread, 1.0, 0.0).astype(jnp.bfloat16)
        across = lax.dot_general(
            folded, spread, (((0,), (0,)), ((), ())), preferred_element_type=jnp.float32
        )
        column = iota((lines, depth), 1)
        parts = []
        for part in range(2):
            chosen = across[part * half : part * half + lines]
            for k in range(1, band):
                at = part * half + k * lines
                chosen = jnp.where(column % band == k, across[at : at + lines], chosen)
            parts.append(chosen)
        for part in range(2):
            line_ref[part * lines : (part + 1) * lines] = parts[part]
        mine = iota((8, depth), 1) // cycles == iota((8, depth), 0) % owned
        weights = []
        for i in range(lines):
            value = jnp.where(
                iota((8, depth), 0) < owned,
                jnp.broadcast_to(line_ref[i : i + 1], (8, depth)),
                jnp.broadcast_to(line_ref[lines + i : lines + i + 1], (8, depth)),
            )
            weights.append(jnp.where(mine, value, 0.0))
        weights = jnp.concatenate(weights, axis=0).astype(jnp.bfloat16)
        sums = jnp.dot(weights, legendre_ref[...].reshape(depth, degrees), preferred_element_type=jnp.float32)

        mode = aux_ref[4].astype(jnp.int32)
        degree = lax.axis_index("lblk") * degrees + lane
        even = ((degree + mode) & 1) == 0
        beyond = degree - mode
        for j in range(0, columns, 2):
            inside = [beyond >= -(j + i) * LANES for i in range(2)]
            for x in range(maps):
                near, far = (
                    jnp.where(
                        inside[i],
                        jnp.where(
                            even,
                            sums[x * 8 : x * 8 + 8, (j + i) * LANES : (j + i + 1) * LANES],
                            sums[(maps + x) * 8 : (maps + x) * 8 + 8, (j + i) * LANES : (j + i + 1) * LANES],
                        ),
                        0.0,
                    )
                    for i in range(2)
                )
                at = (x * 2 * columns + j) * owned
                out_ref[pl.ds(at, 8)] = jnp.where(lower, near, pltpu.roll(far, owned, 0))
                at += columns * owned
                out_ref[pl.ds(at, 8)] = jnp.where(lower, pltpu.roll(near, owned, 0), far)

    return body


def on_chip(value):
    return pltpu.with_memory_space_constraint(value, pltpu.VMEM)


def local(sky, arc_start, arc_count, owner_modes, legendre):
    maps, _, band, quarter = sky.shape
    slots = owner_modes.shape[0]
    owned, groups, _, degrees = legendre.shape
    blocks, copies = lax.axis_size("blk"), lax.axis_size("lblk")
    ring = quarter * copies
    chunk = min(slots, LANES // 4)
    chunks = slots // chunk
    room = pltpu.CompilerParams(vmem_limit_bytes=28 * 2**20 if chunks > 1 else None)
    pieces = quarter // LANES
    sky_rows = sky.reshape(maps, 2, band, pieces, LANES).transpose(0, 1, 3, 2, 4)
    sky_rows = sky_rows.reshape(maps * 2 * pieces * band, LANES)
    scalars = pl.BlockSpec(memory_space=pltpu.SMEM)
    whole = pl.BlockSpec(memory_space=pltpu.VMEM)
    mask, table, turn, aux = pl.pallas_call(
        table_kernel(band, quarter, ring, owned, chunk),
        out_shape=(
            pltpu.VMEM((2 * pieces * band, LANES), jnp.bfloat16),
            pltpu.VMEM((chunks, LANES, 4 * chunk), jnp.bfloat16),
            pltpu.VMEM((chunks, pieces * band, 4 * chunk), jnp.float32),
            pltpu.VMEM((5, 8, LANES), jnp.float32),
        ),
        in_specs=[scalars] * 3 + [whole],
        out_specs=(whole,) * 4,
        cost_estimate=pl.CostEstimate(flops=10**9, bytes_accessed=4 * 10**6, transcendentals=10**6),
        compiler_params=room,
        name="tables",
    )(arc_start, arc_count, owner_modes, owner_modes.reshape(chunks, 1, chunk))
    partial = pl.pallas_call(
        fourier_kernel(maps, band, pieces, owned, copies, chunk, chunks, STEP),
        out_shape=pltpu.VMEM((blocks * copies * owned, LANES), jnp.float32),
        in_specs=[whole] * 4,
        out_specs=whole,
        scratch_shapes=[pltpu.VMEM((8 * 2 * maps, LANES), jnp.float32)],
        compiler_params=room,
        name="fourier",
    )(*(on_chip(v) for v in (sky_rows, mask, table, turn)))
    partial = partial.reshape(blocks * copies, owned, LANES)
    received = lax.all_to_all(partial, ("blk", "lblk"), split_axis=0, concat_axis=0, tiled=True)
    legendre_rows = legendre.reshape(owned * groups, band, degrees)
    received = received.reshape(blocks * copies * owned, LANES)
    columns = degrees // LANES
    result = pl.pallas_call(
        legendre_kernel(maps, band, owned, blocks, copies, degrees, ring),
        out_shape=jax.ShapeDtypeStruct((maps * 2 * columns * owned, LANES), jnp.float32),
        in_specs=[whole] * 3,
        out_specs=whole,
        scratch_shapes=[pltpu.VMEM((4 * maps, owned * groups * band), jnp.float32)],
        compiler_params=room,
        name="legendre",
    )(on_chip(received), on_chip(aux), on_chip(legendre_rows))
    result = result.reshape(maps, 2, columns, owned, LANES).transpose(0, 1, 3, 2, 4)
    return result.reshape(maps, 2, owned, degrees)


def solution(mesh):
    return jax.shard_map(
        local,
        mesh=mesh,
        in_specs=(
            P(None, None, "blk", "lblk"),
            P(None, "blk"),
            P(None, "blk"),
            P(),
            P("blk", None, None, "lblk"),
        ),
        out_specs=P(None, None, "blk", "lblk"),
        check_vma=False,
    )
```

```python
import math

import jax
import jax.numpy as jnp
from jax import lax
from jax.experimental import pallas as pl
from jax.experimental.pallas import tpu as pltpu
from jax.sharding import PartitionSpec as P

DIFFUSION = 0.2
LANES = 128
STEP = 4

COS_TERMS = (1.0, -1.0 / 2, 1.0 / 24, -1.0 / 720, 1.0 / 40320, -1.0 / 3628800)
SIN_TERMS = (1.0, -1.0 / 6, 1.0 / 120, -1.0 / 5040, 1.0 / 362880)


def horner(terms, square):
    total = jnp.full_like(square, terms[-1])
    for term in terms[-2::-1]:
        total = total * square + term
    return total


def circle(index, turn):
    index = index & (turn - 1)
    quadrant = (index * 4 + turn // 2) >> (turn.bit_length() - 1)
    rest = (index - quadrant * (turn // 4)).astype(jnp.float32) * (2.0 * math.pi / turn)
    square = rest * rest
    cosine = horner(COS_TERMS, square)
    sine = rest * horner(SIN_TERMS, square)
    odd = (quadrant & 1) == 1
    swapped_cos = jnp.where(odd, sine, cosine)
    swapped_sin = jnp.where(odd, cosine, sine)
    cos_sign = ((quadrant + 1) & 2) == 2
    sin_sign = (quadrant & 2) == 2
    return (
        jnp.where(cos_sign, -swapped_cos, swapped_cos),
        jnp.where(sin_sign, -swapped_sin, swapped_sin),
    )


def iota(shape, axis):
    return lax.broadcasted_iota(jnp.int32, shape, axis)


def powers(first, count):
    return [first << i for i in range(count.bit_length() - 1)]


def rotations(index, lane_modes, ring):
    amount = jnp.zeros((len(index), 1), jnp.int32)
    for i, value in enumerate(index):
        amount = jnp.where(iota(amount.shape, 0) == i, value, amount)
    return circle(amount * lane_modes, ring)


def unrolled(first, second, cosines, sines):
    blocks = [(first, second)]
    for i in range(cosines.shape[0]):
        cosine, sine = cosines[i : i + 1], sines[i : i + 1]
        blocks += [(f * cosine - s * sine, s * cosine + f * sine) for f, s in blocks]
    return [f for f, _ in blocks]


def table_kernel(band, quarter, ring, owned, chunk):
    pieces = quarter // LANES
    width = 4 * chunk

    def body(start_ref, count_ref, modes_ref, lane_modes_ref, mask_ref, table_ref, turn_ref, aux_ref):
        first_pixel = lax.axis_index("lblk") * quarter
        block = lax.axis_index("blk")
        row = iota((8, LANES), 0)
        lane = iota((8, LANES), 1)
        mine = jnp.zeros((8, LANES), jnp.int32)
        for s in range(owned):
            mine = jnp.where(row % owned == s, modes_ref[block * owned + s], mine)
        half = LANES // 2
        odd = (lane // (half // band)) % band % 2
        scale = DIFFUSION / math.sqrt(ring)
        step_cos, _ = circle(mine, ring)
        turn_cos, turn_sin = circle(mine * odd, 2 * ring)
        turn_sin = jnp.where(lane < half, turn_sin, -turn_sin)
        centre = scale * (1.0 + 2.0 * step_cos)
        aux_ref[0] = turn_cos * centre
        aux_ref[1] = turn_cos * scale
        aux_ref[2] = turn_sin * centre
        aux_ref[3] = turn_sin * scale
        aux_ref[4] = mine.astype(jnp.float32)

        masks = []
        for h in range(2):
            start = jnp.zeros((8, LANES), jnp.int32)
            count = jnp.zeros((8, LANES), jnp.int32)
            for k in range(band):
                start = jnp.where(row % band == k, start_ref[h, k], start)
                count = jnp.where(row % band == k, count_ref[h, k], count)
            shifted = first_pixel + (row // band) * LANES + lane - start
            for t in range(pieces * band // 8):
                offset = (shifted + t * (8 // band) * LANES) & (ring - 1)
                masks.append(jnp.where(offset < count, 1.0, 0.0))
        mask_ref[...] = jnp.concatenate(masks, axis=0).astype(jnp.bfloat16)

        kind = iota((1, width), 1) // chunk
        step = 8 // band * LANES
        in_table = powers(8, LANES // 8)
        in_turn = powers(step, quarter // step)
        for g in range(lane_modes_ref.shape[0]):
            modes = jnp.concatenate([lane_modes_ref[g]] * 4, axis=1)
            cosines, sines = rotations(in_table + in_turn, modes, ring)
            cosine, sine = circle(iota((8, width), 0) * modes, ring)
            is_cos = kind % 2 == 0
            blocks = unrolled(
                jnp.where(is_cos, cosine, sine),
                jnp.where(is_cos, sine, -cosine),
                cosines[: len(in_table)],
                sines[: len(in_table)],
            )
            table_ref[g] = jnp.concatenate(blocks, axis=0).astype(jnp.bfloat16)
            pixel = first_pixel + iota((8, width), 0) // band * LANES
            cosine, sine = circle(pixel * modes, ring)
            blocks = unrolled(
                jnp.where(kind == 0, cosine, jnp.where(kind == 3, -cosine, -sine)),
                jnp.where(kind == 0, sine, jnp.where(kind == 3, -sine, cosine)),
                cosines[len(in_table) :],
                sines[len(in_table) :],
            )
            turn_ref[g] = jnp.concatenate(blocks, axis=0)

    return body


def fourier_kernel(maps, band, pieces, owned, copies, chunk, chunks, step):
    rows = 2 * pieces * band
    tiles = pieces * band // 8
    lines = 2 * maps
    group = 8 // owned

    def body(sky_ref, mask_ref, table_ref, turn_ref, out_ref, line_ref):
        lower = iota((8, LANES), 0) < owned

        def run(g):
            for first in range(0, maps, step):
                masked = [
                    sky_ref[x * rows : (x + 1) * rows] * mask_ref[...]
                    for x in range(first, first + step)
                ]
                product = jnp.dot(
                    jnp.concatenate(masked, axis=0), table_ref[g], preferred_element_type=jnp.float32
                )
                for x in range(step):
                    totals = []
                    for h in range(2):
                        terms = []
                        for t in range(tiles):
                            at = ((x * 2 + h) * tiles + t) * 8
                            terms.append(product[at : at + 8] * turn_ref[g, t * 8 : t * 8 + 8])
                        while len(terms) > 1:
                            terms = [a + b for a, b in zip(terms[::2], terms[1::2], strict=True)]
                        totals += terms
                    north, south = totals
                    line_ref[pl.ds(first + x, 8, stride=lines)] = north
                    line_ref[pl.ds(maps + first + x, 8, stride=lines)] = south
            gathered = line_ref[: band * lines]
            for piece in range(1, 8 // band):
                gathered = gathered + line_ref[piece * band * lines : (piece + 1) * band * lines]
            turned = gathered.T
            real = turned[:chunk] + turned[chunk : 2 * chunk]
            imag = turned[2 * chunk : 3 * chunk] + turned[3 * chunk :]
            both = jnp.concatenate([real, imag], axis=1)
            tile = copies // group
            for i in range(chunk // 8):
                value = both[i * 8 : i * 8 + 8]
                other = pltpu.roll(value, owned, 0)
                ready = (jnp.where(lower, value, other), jnp.where(lower, other, value))
                for o in range(group):
                    for c in range(tile):
                        at = ((g * (chunk // 8) + i) * group + o) * tile + c
                        out_ref[pl.ds(at * 8, 8)] = ready[o]

        if chunks == 1:
            run(0)
        else:
            lax.fori_loop(0, chunks, lambda g, _: run(g), None)

    return body


def legendre_kernel(maps, band, owned, blocks, copies, degrees, ring):
    cycles = blocks * band
    depth = owned * cycles
    lines = 2 * maps
    half = LANES // 2
    tile = copies * owned // 8
    columns = degrees // LANES

    def body(sums_ref, aux_ref, legendre_ref, out_ref, line_ref):
        lane = iota((8, LANES), 1)
        lower = iota((8, LANES), 0) < owned
        cycle = lane // lines % band
        is_first = cycle == 0
        is_last = cycle == band - 1
        south = lane // maps % 2 == 1

        single = []
        for b in range(blocks):
            total = sums_ref[b * tile * 8 : b * tile * 8 + 8]
            for i in range(1, tile):
                total = total + sums_ref[(b * tile + i) * 8 : (b * tile + i) * 8 + 8]
            single.append(total + pltpu.roll(total, owned, 0))
        none = jnp.zeros((8, LANES), jnp.float32)

        def pair(b):
            at = lambda i: single[i] if 0 <= i < blocks else none
            return jnp.where(lower, at(b), at(b + 1))

        def moved(value, shift):
            return pltpu.roll(value, shift % LANES, 1)

        def opposite(value, shift=0):
            return jnp.where(south, moved(value, shift + maps), moved(value, shift - maps))

        folded = []
        for b in range(0, blocks, 2):
            here = pair(b)
            prior = jnp.where(is_last, pair(b - 1), here)
            later = jnp.where(is_first, pair(b + 1), here)
            swapped = moved(here, half)
            up, up_swapped = moved(prior, lines), moved(prior, lines + half)
            down, down_swapped = moved(later, -lines), moved(later, half - lines)
            above = jnp.where(is_first, up_swapped, up)
            above_swapped = jnp.where(is_first, up, up_swapped)
            below = jnp.where(is_last, down_swapped, down)
            below_swapped = jnp.where(is_last, down, down_swapped)
            if b + 2 == blocks:
                equator = is_last & ~lower
                below = jnp.where(equator, opposite(here), below)
                below_swapped = jnp.where(equator, opposite(here, half), below_swapped)
            fourier = (
                aux_ref[0] * here
                + aux_ref[1] * (above + below)
                + aux_ref[2] * swapped
                + aux_ref[3] * (above_swapped + below_swapped)
            )
            fourier = fourier.astype(jnp.bfloat16).astype(jnp.float32)
            other = opposite(fourier)
            folded.append(jnp.where(south, other - fourier, fourier + other))
        folded = jnp.concatenate(folded, axis=0).astype(jnp.bfloat16)

        row = iota((blocks * owned, depth), 0)
        column = iota((blocks * owned, depth), 1)
        spread = (row // owned == (column // band) % blocks) & (row % owned == column // cycles)
        spread = jnp.where(spread, 1.0, 0.0).astype(jnp.bfloat16)
        across = lax.dot_general(
            folded, spread, (((0,), (0,)), ((), ())), preferred_element_type=jnp.float32
        )
        column = iota((lines, depth), 1)
        parts = []
        for part in range(2):
            chosen = across[part * half : part * half + lines]
            for k in range(1, band):
                at = part * half + k * lines
                chosen = jnp.where(column % band == k, across[at : at + lines], chosen)
            parts.append(chosen)
        for part in range(2):
            line_ref[part * lines : (part + 1) * lines] = parts[part]
        mine = iota((8, depth), 1) // cycles == iota((8, depth), 0) % owned
        weights = []
        for i in range(lines):
            value = jnp.where(
                iota((8, depth), 0) < owned,
                jnp.broadcast_to(line_ref[i : i + 1], (8, depth)),
                jnp.broadcast_to(line_ref[lines + i : lines + i + 1], (8, depth)),
            )
            weights.append(jnp.where(mine, value, 0.0))
        weights = jnp.concatenate(weights, axis=0).astype(jnp.bfloat16)
        sums = jnp.dot(weights, legendre_ref[...].reshape(depth, degrees), preferred_element_type=jnp.float32)

        mode = aux_ref[4].astype(jnp.int32)
        degree = lax.axis_index("lblk") * degrees + lane
        even = ((degree + mode) & 1) == 0
        beyond = degree - mode
        for j in range(0, columns, 2):
            inside = [beyond >= -(j + i) * LANES for i in range(2)]
            for x in range(maps):
                near, far = (
                    jnp.where(
                        inside[i],
                        jnp.where(
                            even,
                            sums[x * 8 : x * 8 + 8, (j + i) * LANES : (j + i + 1) * LANES],
                            sums[(maps + x) * 8 : (maps + x) * 8 + 8, (j + i) * LANES : (j + i + 1) * LANES],
                        ),
                        0.0,
                    )
                    for i in range(2)
                )
                at = (x * 2 * columns + j) * owned
                out_ref[pl.ds(at, 8)] = jnp.where(lower, near, pltpu.roll(far, owned, 0))
                at += columns * owned
                out_ref[pl.ds(at, 8)] = jnp.where(lower, pltpu.roll(near, owned, 0), far)

    return body


def on_chip(value):
    return pltpu.with_memory_space_constraint(value, pltpu.VMEM)


def local(sky, arc_start, arc_count, owner_modes, legendre):
    maps, _, band, quarter = sky.shape
    slots = owner_modes.shape[0]
    owned, groups, _, degrees = legendre.shape
    blocks, copies = lax.axis_size("blk"), lax.axis_size("lblk")
    ring = quarter * copies
    chunk = min(slots, LANES // 4)
    chunks = slots // chunk
    room = pltpu.CompilerParams(vmem_limit_bytes=28 * 2**20 if chunks > 1 else None)
    pieces = quarter // LANES
    sky_rows = sky.reshape(maps, 2, band, pieces, LANES).transpose(0, 1, 3, 2, 4)
    sky_rows = sky_rows.reshape(maps * 2 * pieces * band, LANES)
    scalars = pl.BlockSpec(memory_space=pltpu.SMEM)
    whole = pl.BlockSpec(memory_space=pltpu.VMEM)
    mask, table, turn, aux = pl.pallas_call(
        table_kernel(band, quarter, ring, owned, chunk),
        out_shape=(
            pltpu.VMEM((2 * pieces * band, LANES), jnp.bfloat16),
            pltpu.VMEM((chunks, LANES, 4 * chunk), jnp.bfloat16),
            pltpu.VMEM((chunks, pieces * band, 4 * chunk), jnp.float32),
            pltpu.VMEM((5, 8, LANES), jnp.float32),
        ),
        in_specs=[scalars] * 3 + [whole],
        out_specs=(whole,) * 4,
        cost_estimate=pl.CostEstimate(flops=10**9, bytes_accessed=4 * 10**6, transcendentals=10**6),
        compiler_params=room,
        name="tables",
    )(arc_start, arc_count, owner_modes, owner_modes.reshape(chunks, 1, chunk))
    partial = pl.pallas_call(
        fourier_kernel(maps, band, pieces, owned, copies, chunk, chunks, STEP),
        out_shape=pltpu.VMEM((blocks * copies * owned, LANES), jnp.float32),
        in_specs=[whole] * 4,
        out_specs=whole,
        scratch_shapes=[pltpu.VMEM((8 * 2 * maps, LANES), jnp.float32)],
        compiler_params=room,
        name="fourier",
    )(*(on_chip(v) for v in (sky_rows, mask, table, turn)))
    partial = partial.reshape(blocks * copies, owned, LANES)
    received = lax.all_to_all(partial, ("blk", "lblk"), split_axis=0, concat_axis=0, tiled=True)
    legendre_rows = legendre.reshape(owned * groups, band, degrees)
    received = received.reshape(blocks * copies * owned, LANES)
    columns = degrees // LANES
    result = pl.pallas_call(
        legendre_kernel(maps, band, owned, blocks, copies, degrees, ring),
        out_shape=jax.ShapeDtypeStruct((maps * 2 * columns * owned, LANES), jnp.float32),
        in_specs=[whole] * 3,
        out_specs=whole,
        scratch_shapes=[pltpu.VMEM((4 * maps, owned * groups * band), jnp.float32)],
        compiler_params=room,
        name="legendre",
    )(on_chip(received), on_chip(aux), on_chip(legendre_rows))
    result = result.reshape(maps, 2, columns, owned, LANES).transpose(0, 1, 3, 2, 4)
    return result.reshape(maps, 2, owned, degrees)


def solution(mesh):
    return jax.shard_map(
        local,
        mesh=mesh,
        in_specs=(
            P(None, None, "blk", "lblk"),
            P(None, "blk"),
            P(None, "blk"),
            P(),
            P("blk", None, None, "lblk"),
        ),
        out_specs=P(None, None, "blk", "lblk"),
        check_vma=False,
    )
```

```python
import math

import jax
import jax.numpy as jnp
from jax import lax
from jax.experimental import pallas as pl
from jax.experimental.pallas import tpu as pltpu
from jax.sharding import PartitionSpec as P

DIFFUSION = 0.2
LANES = 128
STEP = 4

COS_TERMS = (1.0, -1.0 / 2, 1.0 / 24, -1.0 / 720, 1.0 / 40320, -1.0 / 3628800)
SIN_TERMS = (1.0, -1.0 / 6, 1.0 / 120, -1.0 / 5040, 1.0 / 362880)


def horner(terms, square):
    total = jnp.full_like(square, terms[-1])
    for term in terms[-2::-1]:
        total = total * square + term
    return total


def circle(index, turn):
    index = index & (turn - 1)
    quadrant = (index * 4 + turn // 2) >> (turn.bit_length() - 1)
    rest = (index - quadrant * (turn // 4)).astype(jnp.float32) * (2.0 * math.pi / turn)
    square = rest * rest
    cosine = horner(COS_TERMS, square)
    sine = rest * horner(SIN_TERMS, square)
    odd = (quadrant & 1) == 1
    swapped_cos = jnp.where(odd, sine, cosine)
    swapped_sin = jnp.where(odd, cosine, sine)
    cos_sign = ((quadrant + 1) & 2) == 2
    sin_sign = (quadrant & 2) == 2
    return (
        jnp.where(cos_sign, -swapped_cos, swapped_cos),
        jnp.where(sin_sign, -swapped_sin, swapped_sin),
    )


def iota(shape, axis):
    return lax.broadcasted_iota(jnp.int32, shape, axis)


def powers(first, count):
    return [first << i for i in range(count.bit_length() - 1)]


def rotations(index, lane_modes, ring):
    amount = jnp.zeros((len(index), 1), jnp.int32)
    for i, value in enumerate(index):
        amount = jnp.where(iota(amount.shape, 0) == i, value, amount)
    return circle(amount * lane_modes, ring)


def unrolled(first, second, cosines, sines):
    blocks = [(first, second)]
    for i in range(cosines.shape[0]):
        cosine, sine = cosines[i : i + 1], sines[i : i + 1]
        blocks += [(f * cosine - s * sine, s * cosine + f * sine) for f, s in blocks]
    return [f for f, _ in blocks]


def table_kernel(band, quarter, ring, owned, chunk):
    pieces = quarter // LANES
    width = 4 * chunk

    def body(start_ref, count_ref, modes_ref, lane_modes_ref, mask_ref, table_ref, turn_ref, aux_ref):
        first_pixel = lax.axis_index("lblk") * quarter
        block = lax.axis_index("blk")
        row = iota((8, LANES), 0)
        lane = iota((8, LANES), 1)
        mine = jnp.zeros((8, LANES), jnp.int32)
        for s in range(owned):
            mine = jnp.where(row % owned == s, modes_ref[block * owned + s], mine)
        half = LANES // 2
        odd = (lane // (half // band)) % band % 2
        scale = DIFFUSION / math.sqrt(ring)
        step_cos, _ = circle(mine, ring)
        turn_cos, turn_sin = circle(mine * odd, 2 * ring)
        turn_sin = jnp.where(lane < half, turn_sin, -turn_sin)
        centre = scale * (1.0 + 2.0 * step_cos)
        aux_ref[0] = turn_cos * centre
        aux_ref[1] = turn_cos * scale
        aux_ref[2] = turn_sin * centre
        aux_ref[3] = turn_sin * scale
        aux_ref[4] = mine.astype(jnp.float32)

        masks = []
        for h in range(2):
            start = jnp.zeros((8, LANES), jnp.int32)
            count = jnp.zeros((8, LANES), jnp.int32)
            for k in range(band):
                start = jnp.where(row % band == k, start_ref[h, k], start)
                count = jnp.where(row % band == k, count_ref[h, k], count)
            shifted = first_pixel + (row // band) * LANES + lane - start
            for t in range(pieces * band // 8):
                offset = (shifted + t * (8 // band) * LANES) & (ring - 1)
                masks.append(jnp.where(offset < count, 1.0, 0.0))
        mask_ref[...] = jnp.concatenate(masks, axis=0).astype(jnp.bfloat16)

        kind = iota((1, width), 1) // chunk
        step = 8 // band * LANES
        in_table = powers(8, LANES // 8)
        in_turn = powers(step, quarter // step)
        for g in range(lane_modes_ref.shape[0]):
            modes = jnp.concatenate([lane_modes_ref[g]] * 4, axis=1)
            cosines, sines = rotations(in_table + in_turn, modes, ring)
            cosine, sine = circle(iota((8, width), 0) * modes, ring)
            is_cos = kind % 2 == 0
            blocks = unrolled(
                jnp.where(is_cos, cosine, sine),
                jnp.where(is_cos, sine, -cosine),
                cosines[: len(in_table)],
                sines[: len(in_table)],
            )
            table_ref[g] = jnp.concatenate(blocks, axis=0).astype(jnp.bfloat16)
            pixel = first_pixel + iota((8, width), 0) // band * LANES
            cosine, sine = circle(pixel * modes, ring)
            blocks = unrolled(
                jnp.where(kind == 0, cosine, jnp.where(kind == 3, -cosine, -sine)),
                jnp.where(kind == 0, sine, jnp.where(kind == 3, -sine, cosine)),
                cosines[len(in_table) :],
                sines[len(in_table) :],
            )
            turn_ref[g] = jnp.concatenate(blocks, axis=0)

    return body


def fourier_kernel(maps, band, pieces, owned, copies, chunk, chunks, step):
    rows = 2 * pieces * band
    tiles = pieces * band // 8
    lines = 2 * maps
    group = 8 // owned

    def body(sky_ref, mask_ref, table_ref, turn_ref, out_ref, line_ref):
        lower = iota((8, LANES), 0) < owned

        def run(g):
            for first in range(0, maps, step):
                masked = [
                    sky_ref[x * rows : (x + 1) * rows] * mask_ref[...]
                    for x in range(first, first + step)
                ]
                product = jnp.dot(
                    jnp.concatenate(masked, axis=0), table_ref[g], preferred_element_type=jnp.float32
                )
                for x in range(step):
                    totals = []
                    for h in range(2):
                        terms = []
                        for t in range(tiles):
                            at = ((x * 2 + h) * tiles + t) * 8
                            terms.append(product[at : at + 8] * turn_ref[g, t * 8 : t * 8 + 8])
                        while len(terms) > 1:
                            terms = [a + b for a, b in zip(terms[::2], terms[1::2], strict=True)]
                        totals += terms
                    north, south = totals
                    line_ref[pl.ds(first + x, 8, stride=lines)] = north
                    line_ref[pl.ds(maps + first + x, 8, stride=lines)] = south
            gathered = line_ref[: band * lines]
            for piece in range(1, 8 // band):
                gathered = gathered + line_ref[piece * band * lines : (piece + 1) * band * lines]
            turned = gathered.T
            real = turned[:chunk] + turned[chunk : 2 * chunk]
            imag = turned[2 * chunk : 3 * chunk] + turned[3 * chunk :]
            both = jnp.concatenate([real, imag], axis=1)
            tile = copies // group
            for i in range(chunk // 8):
                value = both[i * 8 : i * 8 + 8]
                other = pltpu.roll(value, owned, 0)
                ready = (jnp.where(lower, value, other), jnp.where(lower, other, value))
                for o in range(group):
                    for c in range(tile):
                        at = ((g * (chunk // 8) + i) * group + o) * tile + c
                        out_ref[pl.ds(at * 8, 8)] = ready[o]

        if chunks == 1:
            run(0)
        else:
            lax.fori_loop(0, chunks, lambda g, _: run(g), None)

    return body


def legendre_kernel(maps, band, owned, blocks, copies, degrees, ring):
    cycles = blocks * band
    depth = owned * cycles
    lines = 2 * maps
    half = LANES // 2
    tile = copies * owned // 8
    columns = degrees // LANES

    def body(sums_ref, aux_ref, legendre_ref, out_ref, line_ref):
        lane = iota((8, LANES), 1)
        lower = iota((8, LANES), 0) < owned
        cycle = lane // lines % band
        is_first = cycle == 0
        is_last = cycle == band - 1
        south = lane // maps % 2 == 1

        single = []
        for b in range(blocks):
            total = sums_ref[b * tile * 8 : b * tile * 8 + 8]
            for i in range(1, tile):
                total = total + sums_ref[(b * tile + i) * 8 : (b * tile + i) * 8 + 8]
            single.append(total + pltpu.roll(total, owned, 0))
        none = jnp.zeros((8, LANES), jnp.float32)

        def pair(b):
            at = lambda i: single[i] if 0 <= i < blocks else none
            return jnp.where(lower, at(b), at(b + 1))

        def moved(value, shift):
            return pltpu.roll(value, shift % LANES, 1)

        def opposite(value, shift=0):
            return jnp.where(south, moved(value, shift + maps), moved(value, shift - maps))

        folded = []
        for b in range(0, blocks, 2):
            here = pair(b)
            prior = jnp.where(is_last, pair(b - 1), here)
            later = jnp.where(is_first, pair(b + 1), here)
            swapped = moved(here, half)
            up, up_swapped = moved(prior, lines), moved(prior, lines + half)
            down, down_swapped = moved(later, -lines), moved(later, half - lines)
            above = jnp.where(is_first, up_swapped, up)
            above_swapped = jnp.where(is_first, up, up_swapped)
            below = jnp.where(is_last, down_swapped, down)
            below_swapped = jnp.where(is_last, down, down_swapped)
            if b + 2 == blocks:
                equator = is_last & ~lower
                below = jnp.where(equator, opposite(here), below)
                below_swapped = jnp.where(equator, opposite(here, half), below_swapped)
            fourier = (
                aux_ref[0] * here
                + aux_ref[1] * (above + below)
                + aux_ref[2] * swapped
                + aux_ref[3] * (above_swapped + below_swapped)
            )
            fourier = fourier.astype(jnp.bfloat16).astype(jnp.float32)
            other = opposite(fourier)
            folded.append(jnp.where(south, other - fourier, fourier + other))
        folded = jnp.concatenate(folded, axis=0).astype(jnp.bfloat16)

        row = iota((blocks * owned, depth), 0)
        column = iota((blocks * owned, depth), 1)
        spread = (row // owned == (column // band) % blocks) & (row % owned == column // cycles)
        spread = jnp.where(spread, 1.0, 0.0).astype(jnp.bfloat16)
        across = lax.dot_general(
            folded, spread, (((0,), (0,)), ((), ())), preferred_element_type=jnp.float32
        )
        column = iota((lines, depth), 1)
        parts = []
        for part in range(2):
            chosen = across[part * half : part * half + lines]
            for k in range(1, band):
                at = part * half + k * lines
                chosen = jnp.where(column % band == k, across[at : at + lines], chosen)
            parts.append(chosen)
        for part in range(2):
            line_ref[part * lines : (part + 1) * lines] = parts[part]
        mine = iota((8, depth), 1) // cycles == iota((8, depth), 0) % owned
        weights = []
        for i in range(lines):
            value = jnp.where(
                iota((8, depth), 0) < owned,
                jnp.broadcast_to(line_ref[i : i + 1], (8, depth)),
                jnp.broadcast_to(line_ref[lines + i : lines + i + 1], (8, depth)),
            )
            weights.append(jnp.where(mine, value, 0.0))
        weights = jnp.concatenate(
            [jnp.concatenate(weights[:maps], axis=0), jnp.concatenate(weights[maps:], axis=0)], axis=1
        ).astype(jnp.bfloat16)

        mode = aux_ref[4].astype(jnp.int32)
        degree = lax.axis_index("lblk") * degrees + iota((8, degrees), 1)
        mode = jnp.concatenate([mode] * columns, axis=1)
        inside = degree >= mode
        even = ((degree + mode) & 1) == 0
        given = legendre_ref[...].reshape(depth, degrees)
        height = depth // owned
        rows = []
        for keep in (inside & even, inside & ~even):
            keep = jnp.where(keep, 1.0, 0.0)
            for s in range(owned):
                factor = jnp.broadcast_to(keep[s : s + 1], (height, degrees)).astype(jnp.bfloat16)
                rows.append(given[s * height : (s + 1) * height] * factor)
        sums = jnp.dot(weights, jnp.concatenate(rows, axis=0), preferred_element_type=jnp.float32)
        for j in range(0, columns, 2):
            for x in range(maps):
                near = sums[x * 8 : x * 8 + 8, j * LANES : (j + 1) * LANES]
                far = sums[x * 8 : x * 8 + 8, (j + 1) * LANES : (j + 2) * LANES]
                at = (x * 2 * columns + j) * owned
                out_ref[pl.ds(at, 8)] = jnp.where(lower, near, pltpu.roll(far, owned, 0))
                at += columns * owned
                out_ref[pl.ds(at, 8)] = jnp.where(lower, pltpu.roll(near, owned, 0), far)

    return body


def on_chip(value):
    return pltpu.with_memory_space_constraint(value, pltpu.VMEM)


def local(sky, arc_start, arc_count, owner_modes, legendre):
    maps, _, band, quarter = sky.shape
    slots = owner_modes.shape[0]
    owned, groups, _, degrees = legendre.shape
    blocks, copies = lax.axis_size("blk"), lax.axis_size("lblk")
    ring = quarter * copies
    chunk = min(slots, LANES // 4)
    chunks = slots // chunk
    room = pltpu.CompilerParams(vmem_limit_bytes=28 * 2**20 if chunks > 1 else None)
    pieces = quarter // LANES
    sky_rows = sky.reshape(maps, 2, band, pieces, LANES).transpose(0, 1, 3, 2, 4)
    sky_rows = sky_rows.reshape(maps * 2 * pieces * band, LANES)
    scalars = pl.BlockSpec(memory_space=pltpu.SMEM)
    whole = pl.BlockSpec(memory_space=pltpu.VMEM)
    mask, table, turn, aux = pl.pallas_call(
        table_kernel(band, quarter, ring, owned, chunk),
        out_shape=(
            pltpu.VMEM((2 * pieces * band, LANES), jnp.bfloat16),
            pltpu.VMEM((chunks, LANES, 4 * chunk), jnp.bfloat16),
            pltpu.VMEM((chunks, pieces * band, 4 * chunk), jnp.float32),
            pltpu.VMEM((5, 8, LANES), jnp.float32),
        ),
        in_specs=[scalars] * 3 + [whole],
        out_specs=(whole,) * 4,
        cost_estimate=pl.CostEstimate(flops=10**9, bytes_accessed=4 * 10**6, transcendentals=10**6),
        compiler_params=room,
        name="tables",
    )(arc_start, arc_count, owner_modes, owner_modes.reshape(chunks, 1, chunk))
    partial = pl.pallas_call(
        fourier_kernel(maps, band, pieces, owned, copies, chunk, chunks, STEP),
        out_shape=pltpu.VMEM((blocks * copies * owned, LANES), jnp.float32),
        in_specs=[whole] * 4,
        out_specs=whole,
        scratch_shapes=[pltpu.VMEM((8 * 2 * maps, LANES), jnp.float32)],
        compiler_params=room,
        name="fourier",
    )(*(on_chip(v) for v in (sky_rows, mask, table, turn)))
    partial = partial.reshape(blocks * copies, owned, LANES)
    received = lax.all_to_all(partial, ("blk", "lblk"), split_axis=0, concat_axis=0, tiled=True)
    legendre_rows = legendre.reshape(owned * groups, band, degrees)
    received = received.reshape(blocks * copies * owned, LANES)
    columns = degrees // LANES
    result = pl.pallas_call(
        legendre_kernel(maps, band, owned, blocks, copies, degrees, ring),
        out_shape=jax.ShapeDtypeStruct((maps * 2 * columns * owned, LANES), jnp.float32),
        in_specs=[whole] * 3,
        out_specs=whole,
        scratch_shapes=[pltpu.VMEM((4 * maps, owned * groups * band), jnp.float32)],
        compiler_params=room,
        name="legendre",
    )(on_chip(received), on_chip(aux), on_chip(legendre_rows))
    result = result.reshape(maps, 2, columns, owned, LANES).transpose(0, 1, 3, 2, 4)
    return result.reshape(maps, 2, owned, degrees)


def solution(mesh):
    return jax.shard_map(
        local,
        mesh=mesh,
        in_specs=(
            P(None, None, "blk", "lblk"),
            P(None, "blk"),
            P(None, "blk"),
            P(),
            P("blk", None, None, "lblk"),
        ),
        out_specs=P(None, None, "blk", "lblk"),
        check_vma=False,
    )
```

```python
import math

import jax
import jax.numpy as jnp
from jax import lax
from jax.experimental import pallas as pl
from jax.experimental.pallas import tpu as pltpu
from jax.sharding import PartitionSpec as P

DIFFUSION = 0.2
LANES = 128
STEP = 4

COS_TERMS = (1.0, -1.0 / 2, 1.0 / 24, -1.0 / 720, 1.0 / 40320, -1.0 / 3628800)
SIN_TERMS = (1.0, -1.0 / 6, 1.0 / 120, -1.0 / 5040, 1.0 / 362880)


def horner(terms, square):
    total = jnp.full_like(square, terms[-1])
    for term in terms[-2::-1]:
        total = total * square + term
    return total


def circle(index, turn):
    index = index & (turn - 1)
    quadrant = (index * 4 + turn // 2) >> (turn.bit_length() - 1)
    rest = (index - quadrant * (turn // 4)).astype(jnp.float32) * (2.0 * math.pi / turn)
    square = rest * rest
    cosine = horner(COS_TERMS, square)
    sine = rest * horner(SIN_TERMS, square)
    odd = (quadrant & 1) == 1
    swapped_cos = jnp.where(odd, sine, cosine)
    swapped_sin = jnp.where(odd, cosine, sine)
    cos_sign = ((quadrant + 1) & 2) == 2
    sin_sign = (quadrant & 2) == 2
    return (
        jnp.where(cos_sign, -swapped_cos, swapped_cos),
        jnp.where(sin_sign, -swapped_sin, swapped_sin),
    )


def iota(shape, axis):
    return lax.broadcasted_iota(jnp.int32, shape, axis)


def powers(first, count):
    return [first << i for i in range(count.bit_length() - 1)]


def rotations(index, lane_modes, ring):
    amount = jnp.zeros((len(index), 1), jnp.int32)
    for i, value in enumerate(index):
        amount = jnp.where(iota(amount.shape, 0) == i, value, amount)
    return circle(amount * lane_modes, ring)


def unrolled(first, second, cosines, sines):
    blocks = [(first, second)]
    for i in range(cosines.shape[0]):
        cosine, sine = cosines[i : i + 1], sines[i : i + 1]
        blocks += [(f * cosine - s * sine, s * cosine + f * sine) for f, s in blocks]
    return [f for f, _ in blocks]


def table_kernel(band, quarter, ring, owned, chunk):
    pieces = quarter // LANES
    width = 4 * chunk

    def body(start_ref, count_ref, modes_ref, lane_modes_ref, mask_ref, table_ref, turn_ref, aux_ref):
        first_pixel = lax.axis_index("lblk") * quarter
        block = lax.axis_index("blk")
        row = iota((8, LANES), 0)
        lane = iota((8, LANES), 1)
        mine = jnp.zeros((8, LANES), jnp.int32)
        for s in range(owned):
            mine = jnp.where(row % owned == s, modes_ref[block * owned + s], mine)
        half = LANES // 2
        odd = (lane // (half // band)) % band % 2
        scale = DIFFUSION / math.sqrt(ring)
        step_cos, _ = circle(mine, ring)
        turn_cos, turn_sin = circle(mine * odd, 2 * ring)
        turn_sin = jnp.where(lane < half, turn_sin, -turn_sin)
        centre = scale * (1.0 + 2.0 * step_cos)
        aux_ref[0] = turn_cos * centre
        aux_ref[1] = turn_cos * scale
        aux_ref[2] = turn_sin * centre
        aux_ref[3] = turn_sin * scale
        aux_ref[4] = mine.astype(jnp.float32)

        masks = []
        for h in range(2):
            start = jnp.zeros((8, LANES), jnp.int32)
            count = jnp.zeros((8, LANES), jnp.int32)
            for k in range(band):
                start = jnp.where(row % band == k, start_ref[h, k], start)
                count = jnp.where(row % band == k, count_ref[h, k], count)
            shifted = first_pixel + (row // band) * LANES + lane - start
            for t in range(pieces * band // 8):
                offset = (shifted + t * (8 // band) * LANES) & (ring - 1)
                masks.append(jnp.where(offset < count, 1.0, 0.0))
        mask_ref[...] = jnp.concatenate(masks, axis=0).astype(jnp.bfloat16)

        kind = iota((1, width), 1) // chunk
        step = 8 // band * LANES
        in_table = powers(8, LANES // 8)
        in_turn = powers(step, quarter // step)
        for g in range(lane_modes_ref.shape[0]):
            modes = jnp.concatenate([lane_modes_ref[g]] * 4, axis=1)
            cosines, sines = rotations(in_table + in_turn, modes, ring)
            cosine, sine = circle(iota((8, width), 0) * modes, ring)
            is_cos = kind % 2 == 0
            blocks = unrolled(
                jnp.where(is_cos, cosine, sine),
                jnp.where(is_cos, sine, -cosine),
                cosines[: len(in_table)],
                sines[: len(in_table)],
            )
            table_ref[g] = jnp.concatenate(blocks, axis=0).astype(jnp.bfloat16)
            pixel = first_pixel + iota((8, width), 0) // band * LANES
            cosine, sine = circle(pixel * modes, ring)
            blocks = unrolled(
                jnp.where(kind == 0, cosine, jnp.where(kind == 3, -cosine, -sine)),
                jnp.where(kind == 0, sine, jnp.where(kind == 3, -sine, cosine)),
                cosines[len(in_table) :],
                sines[len(in_table) :],
            )
            turn_ref[g] = jnp.concatenate(blocks, axis=0)

    return body


def fourier_kernel(maps, band, pieces, owned, copies, chunk, chunks, step):
    rows = 2 * pieces * band
    tiles = pieces * band // 8
    lines = 2 * maps
    group = 8 // owned

    def body(sky_ref, mask_ref, table_ref, turn_ref, out_ref, line_ref):
        lower = iota((8, LANES), 0) < owned

        def run(g):
            for first in range(0, maps, step):
                masked = [
                    sky_ref[x * rows : (x + 1) * rows] * mask_ref[...]
                    for x in range(first, first + step)
                ]
                product = jnp.dot(
                    jnp.concatenate(masked, axis=0), table_ref[g], preferred_element_type=jnp.float32
                )
                for x in range(step):
                    totals = []
                    for h in range(2):
                        terms = []
                        for t in range(tiles):
                            at = ((x * 2 + h) * tiles + t) * 8
                            terms.append(product[at : at + 8] * turn_ref[g, t * 8 : t * 8 + 8])
                        while len(terms) > 1:
                            terms = [a + b for a, b in zip(terms[::2], terms[1::2], strict=True)]
                        totals += terms
                    north, south = totals
                    line_ref[pl.ds(first + x, 8, stride=lines)] = north + south
                    line_ref[pl.ds(maps + first + x, 8, stride=lines)] = north - south
            gathered = line_ref[: band * lines]
            for piece in range(1, 8 // band):
                gathered = gathered + line_ref[piece * band * lines : (piece + 1) * band * lines]
            turned = gathered.T
            real = turned[:chunk] + turned[chunk : 2 * chunk]
            imag = turned[2 * chunk : 3 * chunk] + turned[3 * chunk :]
            both = jnp.concatenate([real, imag], axis=1)
            tile = copies // group
            for i in range(chunk // 8):
                value = both[i * 8 : i * 8 + 8]
                other = pltpu.roll(value, owned, 0)
                ready = (jnp.where(lower, value, other), jnp.where(lower, other, value))
                for o in range(group):
                    for c in range(tile):
                        at = ((g * (chunk // 8) + i) * group + o) * tile + c
                        out_ref[pl.ds(at * 8, 8)] = ready[o]

        if chunks == 1:
            run(0)
        else:
            lax.fori_loop(0, chunks, lambda g, _: run(g), None)

    return body


def legendre_kernel(maps, band, owned, blocks, copies, degrees, ring):
    cycles = blocks * band
    depth = owned * cycles
    lines = 2 * maps
    half = LANES // 2
    tile = copies * owned // 8
    columns = degrees // LANES

    def body(sums_ref, aux_ref, legendre_ref, out_ref, line_ref):
        lane = iota((8, LANES), 1)
        lower = iota((8, LANES), 0) < owned
        cycle = lane // lines % band
        is_first = cycle == 0
        is_last = cycle == band - 1
        mirror = jnp.where(lane // maps % 2 == 0, 1.0, -1.0)

        single = []
        for b in range(blocks):
            total = sums_ref[b * tile * 8 : b * tile * 8 + 8]
            for i in range(1, tile):
                total = total + sums_ref[(b * tile + i) * 8 : (b * tile + i) * 8 + 8]
            single.append(total + pltpu.roll(total, owned, 0))
        none = jnp.zeros((8, LANES), jnp.float32)

        def pair(b):
            at = lambda i: single[i] if 0 <= i < blocks else none
            return jnp.where(lower, at(b), at(b + 1))

        def moved(value, shift):
            return pltpu.roll(value, shift % LANES, 1)

        folded = []
        for b in range(0, blocks, 2):
            here = pair(b)
            prior = jnp.where(is_last, pair(b - 1), here)
            later = jnp.where(is_first, pair(b + 1), here)
            swapped = moved(here, half)
            up, up_swapped = moved(prior, lines), moved(prior, lines + half)
            down, down_swapped = moved(later, -lines), moved(later, half - lines)
            above = jnp.where(is_first, up_swapped, up)
            above_swapped = jnp.where(is_first, up, up_swapped)
            below = jnp.where(is_last, down_swapped, down)
            below_swapped = jnp.where(is_last, down, down_swapped)
            if b + 2 == blocks:
                equator = is_last & ~lower
                below = jnp.where(equator, mirror * here, below)
                below_swapped = jnp.where(equator, mirror * swapped, below_swapped)
            folded.append(
                aux_ref[0] * here
                + aux_ref[1] * (above + below)
                + aux_ref[2] * swapped
                + aux_ref[3] * (above_swapped + below_swapped)
            )
        folded = jnp.concatenate(folded, axis=0).astype(jnp.bfloat16)

        row = iota((blocks * owned, depth), 0)
        column = iota((blocks * owned, depth), 1)
        spread = (row // owned == (column // band) % blocks) & (row % owned == column // cycles)
        spread = jnp.where(spread, 1.0, 0.0).astype(jnp.bfloat16)
        across = lax.dot_general(
            folded, spread, (((0,), (0,)), ((), ())), preferred_element_type=jnp.float32
        )
        column = iota((lines, depth), 1)
        parts = []
        for part in range(2):
            chosen = across[part * half : part * half + lines]
            for k in range(1, band):
                at = part * half + k * lines
                chosen = jnp.where(column % band == k, across[at : at + lines], chosen)
            parts.append(chosen)
        for part in range(2):
            line_ref[part * lines : (part + 1) * lines] = parts[part]
        mine = iota((8, depth), 1) // cycles == iota((8, depth), 0) % owned
        weights = []
        for i in range(lines):
            value = jnp.where(
                iota((8, depth), 0) < owned,
                jnp.broadcast_to(line_ref[i : i + 1], (8, depth)),
                jnp.broadcast_to(line_ref[lines + i : lines + i + 1], (8, depth)),
            )
            weights.append(jnp.where(mine, value, 0.0))
        weights = jnp.concatenate(
            [jnp.concatenate(weights[:maps], axis=0), jnp.concatenate(weights[maps:], axis=0)], axis=1
        ).astype(jnp.bfloat16)

        mode = aux_ref[4].astype(jnp.int32)
        degree = lax.axis_index("lblk") * degrees + iota((8, degrees), 1)
        mode = jnp.concatenate([mode] * columns, axis=1)
        inside = degree >= mode
        even = ((degree + mode) & 1) == 0
        given = legendre_ref[...].reshape(depth, degrees)
        height = depth // owned
        rows = []
        for keep in (inside & even, inside & ~even):
            keep = jnp.where(keep, 1.0, 0.0)
            for s in range(owned):
                factor = jnp.broadcast_to(keep[s : s + 1], (height, degrees)).astype(jnp.bfloat16)
                rows.append(given[s * height : (s + 1) * height] * factor)
        sums = jnp.dot(weights, jnp.concatenate(rows, axis=0), preferred_element_type=jnp.float32)
        for j in range(0, columns, 2):
            for x in range(maps):
                near = sums[x * 8 : x * 8 + 8, j * LANES : (j + 1) * LANES]
                far = sums[x * 8 : x * 8 + 8, (j + 1) * LANES : (j + 2) * LANES]
                at = (x * 2 * columns + j) * owned
                out_ref[pl.ds(at, 8)] = jnp.where(lower, near, pltpu.roll(far, owned, 0))
                at += columns * owned
                out_ref[pl.ds(at, 8)] = jnp.where(lower, pltpu.roll(near, owned, 0), far)

    return body


def on_chip(value):
    return pltpu.with_memory_space_constraint(value, pltpu.VMEM)


def local(sky, arc_start, arc_count, owner_modes, legendre):
    maps, _, band, quarter = sky.shape
    slots = owner_modes.shape[0]
    owned, groups, _, degrees = legendre.shape
    blocks, copies = lax.axis_size("blk"), lax.axis_size("lblk")
    ring = quarter * copies
    chunk = min(slots, LANES // 4)
    chunks = slots // chunk
    room = pltpu.CompilerParams(vmem_limit_bytes=28 * 2**20 if chunks > 1 else None)
    pieces = quarter // LANES
    sky_rows = sky.reshape(maps, 2, band, pieces, LANES).transpose(0, 1, 3, 2, 4)
    sky_rows = sky_rows.reshape(maps * 2 * pieces * band, LANES)
    scalars = pl.BlockSpec(memory_space=pltpu.SMEM)
    whole = pl.BlockSpec(memory_space=pltpu.VMEM)
    mask, table, turn, aux = pl.pallas_call(
        table_kernel(band, quarter, ring, owned, chunk),
        out_shape=(
            pltpu.VMEM((2 * pieces * band, LANES), jnp.bfloat16),
            pltpu.VMEM((chunks, LANES, 4 * chunk), jnp.bfloat16),
            pltpu.VMEM((chunks, pieces * band, 4 * chunk), jnp.float32),
            pltpu.VMEM((5, 8, LANES), jnp.float32),
        ),
        in_specs=[scalars] * 3 + [whole],
        out_specs=(whole,) * 4,
        cost_estimate=pl.CostEstimate(flops=10**9, bytes_accessed=4 * 10**6, transcendentals=10**6),
        compiler_params=room,
        name="tables",
    )(arc_start, arc_count, owner_modes, owner_modes.reshape(chunks, 1, chunk))
    partial = pl.pallas_call(
        fourier_kernel(maps, band, pieces, owned, copies, chunk, chunks, STEP),
        out_shape=pltpu.VMEM((blocks * copies * owned, LANES), jnp.float32),
        in_specs=[whole] * 4,
        out_specs=whole,
        scratch_shapes=[pltpu.VMEM((8 * 2 * maps, LANES), jnp.float32)],
        compiler_params=room,
        name="fourier",
    )(*(on_chip(v) for v in (sky_rows, mask, table, turn)))
    partial = partial.reshape(blocks * copies, owned, LANES)
    received = lax.all_to_all(partial, ("blk", "lblk"), split_axis=0, concat_axis=0, tiled=True)
    legendre_rows = legendre.reshape(owned * groups, band, degrees)
    received = received.reshape(blocks * copies * owned, LANES)
    columns = degrees // LANES
    result = pl.pallas_call(
        legendre_kernel(maps, band, owned, blocks, copies, degrees, ring),
        out_shape=jax.ShapeDtypeStruct((maps * 2 * columns * owned, LANES), jnp.float32),
        in_specs=[whole] * 3,
        out_specs=whole,
        scratch_shapes=[pltpu.VMEM((4 * maps, owned * groups * band), jnp.float32)],
        compiler_params=room,
        name="legendre",
    )(on_chip(received), on_chip(aux), on_chip(legendre_rows))
    result = result.reshape(maps, 2, columns, owned, LANES).transpose(0, 1, 3, 2, 4)
    return result.reshape(maps, 2, owned, degrees)


def solution(mesh):
    return jax.shard_map(
        local,
        mesh=mesh,
        in_specs=(
            P(None, None, "blk", "lblk"),
            P(None, "blk"),
            P(None, "blk"),
            P(),
            P("blk", None, None, "lblk"),
        ),
        out_specs=P(None, None, "blk", "lblk"),
        check_vma=False,
    )
```
